256 devices in a mesh: fsdp: 32 (over y, x, core), rep: 8 (over z).
Axes of the slice: x: 4, y: 4, z: 8, core: 2. Of those that a mesh axis runs over, the one named last changes fastest.
Arguments:
- tokens: bfloat16 [8, 4096, 2048], P('rep', 'fsdp'), may hold values from -6 to 6
- upstream: bfloat16 [8, 7168, 4096], P('rep', 'fsdp'), may hold values from -0.25 to 0.25
- weight: bfloat16 [2, 7168, 2048], P(None, 'fsdp'), may hold values from -0.125 to 0.125
- feedback: float32 [8, 2, 7168, 2048], P('rep', None, 'fsdp'), may hold values from -6 to 6
- momentum: float32 [2, 7168, 2048], P(None, 'fsdp', 'rep'), may hold values from -6 to 6
- right_factor: float32 [2, 7168, 64], P(None, 'fsdp'), may hold values from -6 to 6
Outputs:
- feedback_next: float32 [8, 2, 7168, 2048], P('rep', None, 'fsdp')
- momentum_next: float32 [2, 7168, 2048], P(None, 'fsdp', 'rep')
- weight_next: bfloat16 [2, 7168, 2048], P(None, 'fsdp', 'rep')
- right_next: float32 [2, 7168, 64], P(None, 'fsdp')
The draws below stay inside these ranges and needn't reach their ends.
All inputs are finite; a program needn't handle non-finite values.
Results may differ from the reference program's by a relative error of at most 0.0023.
Values may be sent and summed in bfloat16 or wider, within the bound.
A program may use at most 128 MiB of HBM per device.

```python
import jax
import jax.numpy as jnp
from jax import lax

D = 2048
FF = 7168
R = 64
TOKENS = 4096
REPLICAS = 8


def shard_levels(stream_key, dims, pieces, least, largest):
    def one(dim, parts):
        heights = jax.random.uniform(jax.random.fold_in(jax.random.fold_in(stream_key, 6), dim), (parts,), jnp.float32, least / len(pieces), largest / len(pieces))
        return jnp.repeat(jnp.exp(heights), dims[dim] // parts).reshape((-1,) + (1,) * (len(dims) - dim - 1))

    level = one(*pieces[0])
    for cut in pieces[1:]:
        level = level * one(*cut)
    return level


def gaussian(rng, shape, spread, reach, pieces=(), kind=jnp.bfloat16):
    loudness = shard_levels(rng, shape, pieces, -0.22, 0.18) if pieces else 1.0
    entries = jax.random.normal(rng, shape, jnp.float32) * spread * loudness
    return jnp.minimum(jnp.maximum(entries, -reach), reach).astype(kind)


def setup_inputs(seed: int = 0) -> dict:
    keys = jax.random.split(jax.random.key(seed), 7)
    return {
        "tokens": gaussian(keys[0], (REPLICAS, TOKENS, D), 1.0, 6.0, ((0, 8), (1, 32))),
        "upstream": gaussian(keys[1], (REPLICAS, FF, TOKENS), (TOKENS ** -0.5), 0.25, ((0, 8), (1, 32))),
        "weight": gaussian(keys[2], (2, FF, D), D ** -0.5, 0.125, ((1, 32),)),
        "feedback": gaussian(keys[3], (REPLICAS, 2, FF, D), 1.0, 6.0, ((0, 8), (2, 32)), jnp.float32),
        "momentum": gaussian(keys[4], (2, FF, D), 1.0, 6.0, ((1, 32), (2, 8)), jnp.float32),
        "right_factor": gaussian(keys[5], (2, FF, R), 1.0, 6.0, ((1, 32),), jnp.float32),
    }


momentum_decay = 0.9
step_rate = 0.05
highest = lax.Precision.HIGHEST

def silu_pair(gate_pre):
    sigmoid = jax.nn.sigmoid(gate_pre)
    return (gate_pre * sigmoid, sigmoid * (1.0 + gate_pre * (1.0 - sigmoid)))

def orthonormal(factor):
    gram_matrix = jnp.einsum('kdr,kds->krs', factor, factor, precision=highest)
    lower_factor = jnp.linalg.cholesky(gram_matrix)
    return lax.linalg.triangular_solve(lower_factor, factor, left_side=False, lower=True, transpose_a=True)

def reference(tokens, upstream, weight, feedback, momentum, right_factor):
    contract_last = (((1,), (1,)), ((), ()))

    def replica_delta(operands):
        rows_in, cotangent, residue = operands
        gate_pre = lax.dot_general(weight[0].astype(jnp.float32), rows_in.astype(jnp.float32), contract_last, preferred_element_type=jnp.float32)
        up_pre = lax.dot_general(weight[1].astype(jnp.float32), rows_in.astype(jnp.float32), contract_last, preferred_element_type=jnp.float32)
        activated, derivative = silu_pair(gate_pre)
        cotangent_wide = cotangent.astype(jnp.float32)
        grad_gate = (cotangent_wide * up_pre * derivative).astype(jnp.bfloat16)
        grad_up = (cotangent_wide * activated).astype(jnp.bfloat16)
        delta_gate = jnp.dot(grad_gate.astype(jnp.float32), rows_in.astype(jnp.float32), preferred_element_type=jnp.float32) + residue[0]
        delta_up = jnp.dot(grad_up.astype(jnp.float32), rows_in.astype(jnp.float32), preferred_element_type=jnp.float32) + residue[1]
        delta = jnp.stack([delta_gate, delta_up])
        left_part = jnp.einsum('kfd,kfr->kdr', delta, right_factor, precision=highest)
        return (delta, left_part)
    delta, left_parts = lax.map(replica_delta, (tokens, upstream, feedback))
    left_mean = jnp.mean(left_parts, axis=0)
    basis = orthonormal(left_mean)

    def right_part(single):
        return jnp.einsum('kfd,kdr->kfr', single, basis, precision=highest)
    right_next = jnp.mean(lax.map(right_part, delta), axis=0)
    approx = jnp.einsum('kdr,kfr->kfd', basis, right_next, precision=highest)
    feedback_next = delta - approx[None]
    momentum_next = momentum_decay * momentum + approx
    weight_next = (weight.astype(jnp.float32) - step_rate * momentum_next).astype(jnp.bfloat16)
    return (feedback_next, momentum_next, weight_next, right_next)
```

```python
import functools

import jax
import jax.numpy as jnp
from jax import lax
from jax.experimental import pallas as pl
from jax.experimental.pallas import tpu as pltpu
from jax.sharding import PartitionSpec as P

momentum_decay = 0.9
step_rate = 0.05
highest = lax.Precision.HIGHEST
MESH = pl.DeviceIdType.MESH
F32 = jnp.float32
BF16 = jnp.bfloat16

CHUNK = 128
HALF = 64
DIM = 2048
HID = 224
RANK = 64
REPS = 8
SIDE = 4
NT = (((1,), (1,)), ((), ()))

ORDER = [
    (0, 0),
    (3, 0), (1, 0), (0, 3), (0, 1),
    (2, 0),
    (0, 2),
    (3, 3), (1, 1), (1, 3), (3, 1),
    (2, 3), (2, 1),
    (3, 2), (1, 2),
    (2, 2),
]
UNIT = {pos: i for i, pos in enumerate(ORDER)}
UNITS = len(ORDER)


def pick(table, u):
    out = jnp.int32(0)
    for i, v in enumerate(table):
        if v:
            out = out + jnp.where(u == i, jnp.int32(v), jnp.int32(0))
    return out


def step_kernel(
    tok_hbm, up_hbm, w_hbm, fb_hbm, rf_hbm,
    delta_out, left_out, aug_out, p_out,
    slots, acc, w, up, rf, r2t, dh, dl,
    snd_sib, rcv_sib, mine, recv1, s1, recv2, s2, recv3, full, psum, recv4, pfull, aug,
    in_sem, out_sem, ag_send, ag_recv, sib_send, sib_recv,
    a_send, a_recv, b_send, b_recv, c_send, c_recv, z_send, z_recv,
    gz_send, gz_recv, gb_send, gb_recv, gc_send, gc_recv, gs_send, gs_recv,
    pz_send, pz_recv, pg_send, pg_recv,
):
    f = lax.axis_index("fsdp")
    z = lax.axis_index("rep")
    c = lax.rem(f, 2)
    x = lax.rem(lax.div(f, 2), SIDE)
    y = lax.div(f, 2 * SIDE)
    p1 = x * (1 - c) + y * c
    p2 = y * (1 - c) + x * c
    t1 = 2 + 6 * c
    t2 = 8 - 6 * c

    def plane(q1, q2):
        return t1 * lax.rem(p1 + q1, SIDE) + t2 * lax.rem(p2 + q2, SIDE) + c

    def first_peer(off):
        return (plane(off, 0), z)

    def second_peer(off):
        return (plane(0, off), z)

    def rep_peer(off):
        return (f, lax.rem(z + off, REPS))

    sibling = (f + 1 - 2 * c, z)

    def remote(src, dst, ssem, rsem, dev):
        return pltpu.make_async_remote_copy(
            src_ref=src, dst_ref=dst, send_sem=ssem, recv_sem=rsem,
            device_id=dev, device_id_type=MESH,
        )

    load_tok = pltpu.make_async_copy(tok_hbm, slots.at[0, pl.ds(0, CHUNK), :], in_sem.at[0])
    load_tok.start()
    loads = [
        pltpu.make_async_copy(w_hbm, w, in_sem.at[1]),
        pltpu.make_async_copy(up_hbm, up, in_sem.at[2]),
        pltpu.make_async_copy(fb_hbm, acc, in_sem.at[3]),
        pltpu.make_async_copy(rf_hbm, rf, in_sem.at[4]),
    ]
    for copy in loads:
        copy.start()

    barrier = pltpu.get_barrier_semaphore()
    peers = [sibling]
    peers += [first_peer(o) for o in (1, 2, 3)]
    peers += [second_peer(o) for o in (1, 2, 3)]
    peers += [rep_peer(o) for o in range(1, REPS)]
    for dev in peers:
        pl.semaphore_signal(barrier, inc=1, device_id=dev, device_id_type=MESH)
    load_tok.wait()
    pl.semaphore_wait(barrier, len(peers))

    started = []

    def piece(d1, d2, h):
        return slots.at[UNIT[(d1, d2)], pl.ds(HALF * h, HALF), :]

    def send(d1, d2, h, axis, way):
        if axis == 1:
            r1, r2 = (d1 - way) % SIDE, d2
            dev = first_peer(way % SIDE)
        else:
            r1, r2 = d1, (d2 - way) % SIDE
            dev = second_peer(way % SIDE)
        copy = remote(
            piece(d1, d2, h), piece(r1, r2, h),
            ag_send.at[len(started)], ag_recv.at[UNIT[(r1, r2)], h], dev,
        )
        copy.start()
        started.append((d1, d2, h))

    def arrived(d1, d2, h):
        remote(
            piece(d1, d2, h), piece(d1, d2, h),
            ag_send.at[0], ag_recv.at[UNIT[(d1, d2)], h], sibling,
        ).wait_recv()

    def own_rows(u):
        return slots.at[u, pl.ds(0, CHUNK), :]

    def sib_rows(u):
        return slots.at[u, pl.ds(CHUNK, CHUNK), :]

    def share(d1, d2):
        u = UNIT[(d1, d2)]
        remote(own_rows(u), sib_rows(u), sib_send.at[u], sib_recv.at[u], sibling).start()

    send(0, 0, 0, 1, 1)
    send(0, 0, 1, 1, -1)
    share(0, 0)
    send(0, 0, 1, 1, 1)
    send(0, 0, 0, 1, -1)
    for copy in loads:
        copy.wait()

    for k in range(2):
        turned = jnp.transpose(rf[k], (1, 0))
        high = turned.astype(BF16)
        r2t[k, pl.ds(0, RANK), :] = high
        r2t[k, pl.ds(RANK, RANK), :] = (turned - high.astype(F32)).astype(BF16)

    def actions(u):
        if u == 0:
            arrived(3, 0, 0)
            arrived(1, 0, 1)
            send(3, 0, 0, 1, 1)
            send(1, 0, 1, 1, -1)
            send(0, 0, 0, 2, 1)
            send(0, 0, 1, 2, -1)
            send(0, 0, 1, 2, 1)
            send(0, 0, 0, 2, -1)
            send(3, 0, 0, 2, 1)
            send(1, 0, 1, 2, -1)
            send(1, 0, 1, 2, 1)
            send(3, 0, 0, 2, -1)
        if u == 1:
            arrived(3, 0, 1)
            arrived(1, 0, 0)
            share(3, 0)
            share(1, 0)
            arrived(0, 3, 0)
            arrived(0, 1, 1)
            send(0, 3, 0, 2, 1)
            send(0, 1, 1, 2, -1)
            send(3, 0, 1, 2, 1)
            send(1, 0, 0, 2, -1)
            send(1, 0, 0, 2, 1)
            send(3, 0, 1, 2, -1)
        if u == 3:
            arrived(0, 3, 1)
            arrived(0, 1, 0)
            share(0, 3)
            share(0, 1)
        if u == 4:
            arrived(2, 0, 0)
            arrived(2, 0, 1)
            share(2, 0)
            send(2, 0, 0, 2, 1)
            send(2, 0, 1, 2, -1)
        if u == 5:
            arrived(3, 3, 0)
            arrived(1, 1, 1)
            send(3, 3, 0, 2, 1)
            send(1, 1, 1, 2, -1)
            send(2, 0, 1, 2, 1)
            send(2, 0, 0, 2, -1)
        if u == 6:
            arrived(0, 2, 0)
            arrived(0, 2, 1)
            share(0, 2)
        if u == 7:
            arrived(3, 3, 1)
            arrived(1, 1, 0)
            share(3, 3)
            share(1, 1)
        if u == 9:
            arrived(1, 3, 0)
            arrived(3, 1, 1)
            send(1, 3, 0, 2, 1)
            send(3, 1, 1, 2, -1)
            arrived(1, 3, 1)
            arrived(3, 1, 0)
            share(1, 3)
            share(3, 1)
        if u == 10:
            arrived(2, 3, 0)
            arrived(2, 1, 1)
            send(2, 3, 0, 2, 1)
            send(2, 1, 1, 2, -1)
        if u == 11:
            arrived(2, 3, 1)
            arrived(2, 1, 0)
            share(2, 3)
            share(2, 1)
        if u == 13:
            arrived(3, 2, 0)
            arrived(1, 2, 1)
            arrived(3, 2, 1)
            arrived(1, 2, 0)
            share(3, 2)
            share(1, 2)
        if u == 15:
            arrived(2, 2, 0)
            arrived(2, 2, 1)
            share(2, 2)

    acting = (0, 1, 3, 4, 5, 6, 7, 9, 10, 11, 13, 15)
    first_of = [d1 for d1, _ in ORDER]
    second_of = [d2 for _, d2 in ORDER]

    def unit_step(u, carry):
        for i in acting:
            @pl.when(u == i)
            def _(i=i):
                actions(i)

        remote(own_rows(u), sib_rows(u), sib_send.at[u], sib_recv.at[u], sibling).wait_recv()
        d1, d2 = pick(first_of, u), pick(second_of, u)
        mine_f = plane(d1, d2)
        other_f = t2 * lax.rem(p2 + d1, SIDE) + t1 * lax.rem(p1 + d2, SIDE) + (1 - c)
        cot_mine = up[:, pl.ds(pl.multiple_of(mine_f * CHUNK, CHUNK), CHUNK)]
        cot_other = up[:, pl.ds(pl.multiple_of(other_f * CHUNK, CHUNK), CHUNK)]
        cot = jnp.concatenate([cot_mine, cot_other], axis=1).astype(F32)
        rows = slots[u]
        pre = lax.dot_general(w[...], rows, NT, preferred_element_type=F32)
        gate_pre, up_pre = pre[:HID], pre[HID:]
        sig = jax.nn.sigmoid(gate_pre)
        grad_gate = (cot * up_pre * (sig * (1.0 + gate_pre * (1.0 - sig)))).astype(BF16)
        grad_up = (cot * (gate_pre * sig)).astype(BF16)
        grads = jnp.concatenate([grad_gate, grad_up], axis=0)
        acc[...] += jnp.dot(grads, rows, preferred_element_type=F32)
        return carry

    lax.fori_loop(0, UNITS, unit_step, 0)

    assert len(started) == AG_SENDS
    stores = [pltpu.make_async_copy(acc, delta_out, out_sem.at[0])]
    stores[0].start()

    def left_part(k, g, dst):
        cols = pl.ds(pl.multiple_of(512 * g, 512) if not isinstance(g, int) else 512 * g, 512)
        kr = pl.ds(pl.multiple_of(HID * k, 32), HID)
        block = acc[kr, cols]
        high = block.astype(BF16)
        low = (block - high.astype(F32)).astype(BF16)
        dh[kr, cols] = high
        dl[kr, cols] = low
        both = jnp.dot(r2t[k], high, preferred_element_type=F32)
        part = both[:RANK] + both[RANK:]
        part = part + jnp.dot(r2t[k, pl.ds(0, RANK), :], low, preferred_element_type=F32)
        for i in range(4):
            dst[4 * g + i] = part[:, 128 * i : 128 * (i + 1)]

    for g in range(4):
        left_part(1 - c, g, snd_sib)
        remote(
            snd_sib.at[pl.ds(4 * g, 4)], rcv_sib.at[pl.ds(4 * g, 4)],
            a_send.at[g], a_recv.at[g], sibling,
        ).start()
    for g in range(4):
        left_part(c, g, mine)
    for g in range(4):
        remote(
            snd_sib.at[pl.ds(4 * g, 4)], rcv_sib.at[pl.ds(4 * g, 4)],
            a_send.at[g], a_recv.at[g], sibling,
        ).wait()

    def first_copy(off):
        q = lax.rem(p1 + off, SIDE)
        return remote(
            mine.at[pl.ds(4 * q, 4)], recv1.at[off - 1],
            b_send.at[off - 1], b_recv.at[off - 1], first_peer(off),
        )

    for off in (2, 1, 3):
        q = lax.rem(p1 + off, SIDE)
        mine[pl.ds(4 * q, 4)] += rcv_sib[pl.ds(4 * q, 4)]
        first_copy(off).start()
    total = mine[pl.ds(4 * p1, 4)] + rcv_sib[pl.ds(4 * p1, 4)]
    for off in (1, 3, 2):
        first_copy(off).wait_recv()
        total = total + recv1[off - 1]
    s1[...] = total

    def second_copy(off):
        q = lax.rem(p2 + off, SIDE)
        return remote(
            s1.at[q], recv2.at[off - 1],
            c_send.at[off - 1], c_recv.at[off - 1], second_peer(off),
        )

    for off in (2, 1, 3):
        second_copy(off).start()
    total = s1[p2]
    for off in (1, 3, 2):
        second_copy(off).wait_recv()
        total = total + recv2[off - 1]
    s2[...] = total

    far_first = (4, 3, 5, 2, 6, 1, 7)

    def rep_copy(off):
        q = lax.rem(z + off, REPS)
        return remote(
            s2.at[pl.ds(pl.multiple_of(8 * q, 8), 8), :], recv3.at[off - 1],
            z_send.at[off - 1], z_recv.at[off - 1], rep_peer(off),
        )

    for off in far_first:
        rep_copy(off).start()
    total = s2[pl.ds(pl.multiple_of(8 * z, 8), 8), :]
    for off in reversed(far_first):
        rep_copy(off).wait_recv()
        total = total + recv3[off - 1]

    b = 4 * p1 + p2
    own_piece = full.at[c, b, pl.ds(pl.multiple_of(8 * z, 8), 8), :]
    own_piece[...] = total * (1.0 / REPS)

    def rep_gather(off):
        return remote(own_piece, own_piece, gz_send.at[off - 1], gz_recv.at[off - 1], rep_peer(off))

    for off in far_first:
        rep_gather(off).start()
    for off in reversed(far_first):
        rep_gather(off).wait_recv()

    def second_gather(off):
        return remote(
            full.at[c, b], full.at[c, b],
            gb_send.at[off - 1], gb_recv.at[off - 1], second_peer(off),
        )

    for off in (2, 1, 3):
        second_gather(off).start()
    for off in (1, 3, 2):
        second_gather(off).wait_recv()

    def first_gather(off):
        group = full.at[c, pl.ds(4 * p1, 4)]
        return remote(group, group, gc_send.at[off - 1], gc_recv.at[off - 1], first_peer(off))

    def pass_on(off):
        q = lax.rem(p1 + 4 - off, SIDE)
        group = full.at[c, pl.ds(4 * q, 4)]
        return remote(group, group, gs_send.at[off], gs_recv.at[off], sibling)

    for off in (2, 1, 3):
        first_gather(off).start()
    pass_on(0).start()
    for off in (1, 3, 2):
        first_gather(off).wait_recv()
        pass_on(off).start()

    lane = lax.broadcasted_iota(jnp.int32, (RANK, 128), 1)
    row = lax.broadcasted_iota(jnp.int32, (RANK, 128), 0)

    def left_rows(k):
        return jnp.concatenate([full[k, i] for i in range(16)], axis=1)

    def product(k):
        left = left_rows(k)
        high = left.astype(BF16)
        low = (left - high.astype(F32)).astype(BF16)
        kr = pl.ds(pl.multiple_of(HID * k, 32), HID)
        part = lax.dot_general(
            dh[kr, :], jnp.concatenate([high, low], axis=0), NT, preferred_element_type=F32
        )
        part = part + pltpu.roll(part, RANK, 1)
        return part + lax.dot_general(
            dl[kr, :], jnp.concatenate([high, high], axis=0), NT, preferred_element_type=F32
        )

    prod_own = product(c)
    for off in range(4):
        pass_on(off).wait()
    prod_other = product(1 - c)
    wide = lax.broadcasted_iota(jnp.int32, (HID, 128), 1)
    low_lanes = (wide < RANK) == (c == 0)
    psum[pl.ds(0, HID), :] = jnp.where(low_lanes, prod_own, prod_other)
    psum[pl.ds(HID, 32), :] = jnp.zeros((32, 128), F32)

    def p_rows(i):
        return pl.ds(pl.multiple_of(32 * i, 32), 32)

    def p_copy(off):
        q = lax.rem(z + off, REPS)
        return remote(
            psum.at[p_rows(q), :], recv4.at[off - 1],
            pz_send.at[off - 1], pz_recv.at[off - 1], rep_peer(off),
        )

    for off in far_first:
        p_copy(off).start()
    store_left = pltpu.make_async_copy(full, left_out, out_sem.at[1])
    store_left.start()

    for k in range(2):
        left = left_rows(k)
        padded = jnp.concatenate([left, jnp.zeros_like(left)], axis=0)
        gram = lax.dot_general(left, padded, NT, precision=highest, preferred_element_type=F32)
        aug[k] = jnp.where(lane == row + RANK, 1.0, gram)

    def eliminate(j, carry):
        for k in range(2):
            table = aug[k]
            pivot_row = aug[k, pl.ds(j, 1), :]
            at_j = lane == j
            pivot = jnp.sum(jnp.where(at_j[:1], pivot_row, 0.0), axis=1, keepdims=True)
            column = jnp.sum(jnp.where(at_j, table, 0.0), axis=1, keepdims=True)
            inv = lax.rsqrt(pivot)
            scaled = pivot_row * inv
            factor = column * inv
            aug[k] = jnp.where(
                row > j, table - factor * scaled, jnp.where(row == j, scaled, table)
            )
        return carry

    lax.fori_loop(0, RANK // 2, eliminate, 0)

    total = psum[p_rows(z), :]
    for off in reversed(far_first):
        p_copy(off).wait_recv()
        total = total + recv4[off - 1]
    pfull[p_rows(z), :] = total * (1.0 / REPS)

    def p_gather(off):
        group = pfull.at[p_rows(z), :]
        return remote(group, group, pg_send.at[off - 1], pg_recv.at[off - 1], rep_peer(off))

    for off in far_first:
        p_gather(off).start()

    lax.fori_loop(RANK // 2, RANK, eliminate, 0)
    aug_out[...] = aug[...]

    for off in reversed(far_first):
        p_gather(off).wait_recv()
    p_out[...] = pfull[...]

    for i, (d1, d2, h) in enumerate(started):
        remote(
            piece(d1, d2, h), piece(d1, d2, h), ag_send.at[i], ag_recv.at[0, 0], sibling
        ).wait_send()
    for u in range(UNITS):
        remote(own_rows(u), sib_rows(u), sib_send.at[u], sib_recv.at[u], sibling).wait_send()
    for off in (1, 2, 3):
        first_copy(off).wait_send()
        second_copy(off).wait_send()
        second_gather(off).wait_send()
        first_gather(off).wait_send()
    for off in far_first:
        rep_copy(off).wait_send()
        rep_gather(off).wait_send()
        p_copy(off).wait_send()
        p_gather(off).wait_send()
    stores[0].wait()
    store_left.wait()


AG_SENDS = 30


def step_call(tokens, upstream, weight, feedback, right_factor):
    any_space = pl.BlockSpec(memory_space=pl.ANY)
    vmem = pl.BlockSpec(memory_space=pltpu.VMEM)
    dma = pltpu.SemaphoreType.DMA
    return pl.pallas_call(
        step_kernel,
        name="gather_reduce",
        out_shape=(
            jax.ShapeDtypeStruct((2 * HID, DIM), F32),
            jax.ShapeDtypeStruct((2, 16, RANK, 128), F32),
            jax.ShapeDtypeStruct((2, RANK, 128), F32),
            jax.ShapeDtypeStruct((256, 128), F32),
        ),
        in_specs=[any_space] * 5,
        out_specs=(any_space, any_space, vmem, vmem),
        scratch_shapes=[
            pltpu.VMEM((UNITS, 2 * CHUNK, DIM), BF16),
            pltpu.VMEM((2 * HID, DIM), F32),
            pltpu.VMEM((2 * HID, DIM), BF16),
            pltpu.VMEM((HID, 32 * CHUNK), BF16),
            pltpu.VMEM((2, HID, RANK), F32),
            pltpu.VMEM((2, 2 * RANK, HID), BF16),
            pltpu.VMEM((2 * HID, DIM), BF16),
            pltpu.VMEM((2 * HID, DIM), BF16),
            pltpu.VMEM((16, RANK, 128), F32),
            pltpu.VMEM((16, RANK, 128), F32),
            pltpu.VMEM((16, RANK, 128), F32),
            pltpu.VMEM((3, 4, RANK, 128), F32),
            pltpu.VMEM((4, RANK, 128), F32),
            pltpu.VMEM((3, RANK, 128), F32),
            pltpu.VMEM((RANK, 128), F32),
            pltpu.VMEM((7, 8, 128), F32),
            pltpu.VMEM((2, 16, RANK, 128), F32),
            pltpu.VMEM((256, 128), F32),
            pltpu.VMEM((7, 32, 128), F32),
            pltpu.VMEM((256, 128), F32),
            pltpu.VMEM((2, RANK, 128), F32),
            dma((5,)), dma((2,)),
            dma((AG_SENDS,)), dma((UNITS, 2)), dma((UNITS,)), dma((UNITS,)),
            dma((4,)), dma((4,)), dma((3,)), dma((3,)), dma((3,)), dma((3,)), dma((7,)), dma((7,)),
            dma((7,)), dma((7,)), dma((3,)), dma((3,)), dma((3,)), dma((3,)), dma((4,)), dma((4,)),
            dma((7,)), dma((7,)), dma((7,)), dma((7,)),
        ],
        compiler_params=pltpu.CompilerParams(
            collective_id=0, has_side_effects=True, vmem_limit_bytes=60 * 1024 * 1024
        ),
    )(
        tokens.reshape(CHUNK, DIM),
        upstream.reshape(HID, 32 * CHUNK),
        weight.reshape(2 * HID, DIM),
        feedback.reshape(2 * HID, DIM),
        right_factor,
    )


COLS = 256


def finish_kernel(
    z_ref, delta, left, aug, p, momentum, weight, fb_out, mom_out, w_out, right_out, coef
):
    j = pl.program_id(0)

    @pl.when(j == 0)
    def _():
        lane = lax.broadcasted_iota(jnp.int32, (RANK, 128), 1)
        for k in range(2):
            turned = jnp.where(lane < RANK, pltpu.roll(aug[k], RANK, 1), 0.0)
            placed = turned if k == 0 else jnp.where(lane >= RANK, aug[k], 0.0)
            right = lax.dot_general(
                p[pl.ds(0, HID), :], placed, NT, precision=highest, preferred_element_type=F32
            )
            right_out[k] = right
            coef[k] = jnp.dot(right, turned, precision=highest, preferred_element_type=F32)[:, :RANK]

    for k in range(2):
        block = jnp.concatenate([left[k, 0], left[k, 1]], axis=1)
        approx = jnp.dot(coef[k], block, precision=highest, preferred_element_type=F32)
        fb_out[k] = delta[k] - approx

        @pl.when(j == z_ref[0])
        def _(k=k, approx=approx):
            moved = momentum_decay * momentum[k] + approx
            mom_out[k] = moved
            w_out[k] = (weight[k].astype(F32) - step_rate * moved).astype(BF16)


def finish_call(slab, delta, left, aug, p, momentum, weight):
    whole = lambda *shape: pl.BlockSpec(shape, lambda j, s: (0,) * len(shape))
    return pl.pallas_call(
        finish_kernel,
        name="finish",
        grid_spec=pltpu.PrefetchScalarGridSpec(
            num_scalar_prefetch=1,
            grid=(DIM // COLS,),
            in_specs=[
                pl.BlockSpec((2, HID, COLS), lambda j, s: (0, 0, j)),
                pl.BlockSpec((2, 2, RANK, 128), lambda j, s: (0, j, 0, 0)),
                whole(2, RANK, 128),
                whole(256, 128),
                whole(2, HID, COLS),
                pl.BlockSpec((2, HID, COLS), lambda j, s: (0, 0, s[0])),
            ],
            out_specs=[
                pl.BlockSpec((2, HID, COLS), lambda j, s: (0, 0, j)),
                whole(2, HID, COLS),
                whole(2, HID, COLS),
                whole(2, HID, RANK),
            ],
            scratch_shapes=[pltpu.VMEM((2, HID, RANK), F32)],
        ),
        out_shape=(
            jax.ShapeDtypeStruct((2, HID, DIM), F32),
            jax.ShapeDtypeStruct((2, HID, COLS), F32),
            jax.ShapeDtypeStruct((2, HID, COLS), BF16),
            jax.ShapeDtypeStruct((2, HID, RANK), F32),
        ),
        compiler_params=pltpu.CompilerParams(dimension_semantics=("arbitrary",)),
    )(slab, delta, left, aug, p, momentum, weight)


def per_device(tokens, upstream, weight, feedback, momentum, right_factor):
    delta, left, aug, p = step_call(tokens, upstream, weight, feedback, right_factor)
    slab = lax.axis_index("rep").astype(jnp.int32).reshape(1)
    feedback_next, momentum_next, weight_next, right_next = finish_call(
        slab, delta.reshape(2, HID, DIM), left, aug, p, momentum, weight
    )
    return (feedback_next[None], momentum_next, weight_next, right_next)


def solution(mesh):
    placed = (
        P("rep", "fsdp", None),
        P("rep", "fsdp", None),
        P(None, "fsdp", None),
        P("rep", None, "fsdp", None),
        P(None, "fsdp", "rep"),
        P(None, "fsdp", None),
    )
    return jax.shard_map(
        per_device,
        mesh=mesh,
        in_specs=placed,
        out_specs=(
            P("rep", None, "fsdp", None),
            P(None, "fsdp", "rep"),
            P(None, "fsdp", "rep"),
            P(None, "fsdp", None),
        ),
        check_vma=False,
    )
```

```python
import functools

import jax
import jax.numpy as jnp
from jax import lax
from jax.experimental import pallas as pl
from jax.experimental.pallas import tpu as pltpu
from jax.sharding import PartitionSpec as P

momentum_decay = 0.9
step_rate = 0.05
highest = lax.Precision.HIGHEST
MESH = pl.DeviceIdType.MESH
F32 = jnp.float32
BF16 = jnp.bfloat16

CHUNK = 128
HALF = 64
DIM = 2048
HID = 224
RANK = 64
REPS = 8
SIDE = 4
NT = (((1,), (1,)), ((), ()))

ORDER = [
    (0, 0), (3, 0),
    (1, 0), (0, 3),
    (0, 1), (2, 0),
    (0, 2), (3, 3),
    (1, 1), (1, 3),
    (3, 1), (2, 3),
    (2, 1), (3, 2),
    (1, 2), (2, 2),
]
UNIT = {pos: i for i, pos in enumerate(ORDER)}
UNITS = len(ORDER)
PAIRS = UNITS // 2


def pick(table, u):
    out = jnp.int32(0)
    for i, v in enumerate(table):
        if v:
            out = out + jnp.where(u == i, jnp.int32(v), jnp.int32(0))
    return out


def step_kernel(
    tok_hbm, up_hbm, w_hbm, fb_hbm, rf_hbm,
    delta_out, left_out, solve_out, p_out,
    slots, acc, w, up, rf, r2t, dsplit,
    snd_sib, rcv_sib, mine, recv1, s1, recv2, s2, recv3, whole, full, psum, recv4, pfull, aug,
    in_sem, out_sem, ag_send, ag_recv, sib_send, sib_recv,
    a_send, a_recv, b_send, b_recv, c_send, c_recv, z_send, z_recv,
    gz_send, gz_recv, gb_send, gb_recv, gc_send, gc_recv, gs_send, gs_recv,
    pz_send, pz_recv, pg_send, pg_recv,
):
    f = lax.axis_index("fsdp")
    z = lax.axis_index("rep")
    c = lax.rem(f, 2)
    x = lax.rem(lax.div(f, 2), SIDE)
    y = lax.div(f, 2 * SIDE)
    p1 = x * (1 - c) + y * c
    p2 = y * (1 - c) + x * c
    t1 = 2 + 6 * c
    t2 = 8 - 6 * c

    def plane(q1, q2):
        return t1 * lax.rem(p1 + q1, SIDE) + t2 * lax.rem(p2 + q2, SIDE) + c

    def first_peer(off):
        return (plane(off, 0), z)

    def second_peer(off):
        return (plane(0, off), z)

    def rep_peer(off):
        return (f, lax.rem(z + off, REPS))

    sibling = (f + 1 - 2 * c, z)

    def remote(src, dst, ssem, rsem, dev):
        return pltpu.make_async_remote_copy(
            src_ref=src, dst_ref=dst, send_sem=ssem, recv_sem=rsem,
            device_id=dev, device_id_type=MESH,
        )

    load_tok = pltpu.make_async_copy(tok_hbm, slots.at[0, pl.ds(0, CHUNK), :], in_sem.at[0])
    load_tok.start()
    loads = [
        pltpu.make_async_copy(w_hbm, w, in_sem.at[1]),
        pltpu.make_async_copy(up_hbm, up, in_sem.at[2]),
        pltpu.make_async_copy(fb_hbm, acc, in_sem.at[3]),
        pltpu.make_async_copy(rf_hbm, rf, in_sem.at[4]),
    ]
    for copy in loads:
        copy.start()

    barrier = pltpu.get_barrier_semaphore()
    peers = [sibling]
    peers += [first_peer(o) for o in (1, 2, 3)]
    peers += [second_peer(o) for o in (1, 2, 3)]
    peers += [rep_peer(o) for o in range(1, REPS)]
    for dev in peers:
        pl.semaphore_signal(barrier, inc=1, device_id=dev, device_id_type=MESH)
    load_tok.wait()
    pl.semaphore_wait(barrier, len(peers))

    started = []

    def piece(d1, d2, h):
        u = UNIT[(d1, d2)]
        return slots.at[u // 2, pl.ds(2 * CHUNK * (u % 2) + HALF * h, HALF), :]

    def send(d1, d2, h, axis, way):
        if axis == 1:
            r1, r2 = (d1 - way) % SIDE, d2
            dev = first_peer(way % SIDE)
        else:
            r1, r2 = d1, (d2 - way) % SIDE
            dev = second_peer(way % SIDE)
        copy = remote(
            piece(d1, d2, h), piece(r1, r2, h),
            ag_send.at[len(started)], ag_recv.at[UNIT[(r1, r2)], h], dev,
        )
        copy.start()
        started.append((d1, d2, h))

    def arrived(d1, d2, h):
        remote(
            piece(d1, d2, h), piece(d1, d2, h),
            ag_send.at[0], ag_recv.at[UNIT[(d1, d2)], h], sibling,
        ).wait_recv()

    def sib_copy(u, half):
        start = 2 * CHUNK * half
        pair = slots.at[lax.div(u, 2)]
        return remote(
            pair.at[pl.ds(start, CHUNK), :], pair.at[pl.ds(start + CHUNK, CHUNK), :],
            sib_send.at[u], sib_recv.at[u], sibling,
        )

    def share(d1, d2):
        u = UNIT[(d1, d2)]
        sib_copy(u, u % 2).start()

    send(0, 0, 0, 1, 1)
    send(0, 0, 1, 1, -1)
    share(0, 0)
    send(0, 0, 1, 1, 1)
    send(0, 0, 0, 1, -1)
    for copy in loads:
        copy.wait()

    for k in range(2):
        turned = rf[k]
        high = turned.astype(BF16)
        r2t[k, pl.ds(0, RANK), :] = high
        r2t[k, pl.ds(RANK, RANK), :] = (turned - high.astype(F32)).astype(BF16)

    def actions(step):
        if step == 0:
            arrived(3, 0, 0)
            arrived(1, 0, 1)
            send(3, 0, 0, 1, 1)
            send(1, 0, 1, 1, -1)
            send(0, 0, 0, 2, 1)
            send(0, 0, 1, 2, -1)
            send(0, 0, 1, 2, 1)
            send(0, 0, 0, 2, -1)
            send(3, 0, 0, 2, 1)
            send(1, 0, 1, 2, -1)
            send(1, 0, 1, 2, 1)
            send(3, 0, 0, 2, -1)
            arrived(3, 0, 1)
            arrived(1, 0, 0)
            share(3, 0)
            share(1, 0)
            arrived(0, 3, 0)
            arrived(0, 1, 1)
            send(0, 3, 0, 2, 1)
            send(0, 1, 1, 2, -1)
            send(3, 0, 1, 2, 1)
            send(1, 0, 0, 2, -1)
            send(1, 0, 0, 2, 1)
            send(3, 0, 1, 2, -1)
        if step == 1:
            arrived(0, 3, 1)
            arrived(0, 1, 0)
            share(0, 3)
            share(0, 1)
            arrived(2, 0, 0)
            arrived(2, 0, 1)
            send(2, 0, 0, 2, 1)
            send(2, 0, 1, 2, -1)
            share(2, 0)
        if step == 2:
            arrived(3, 3, 0)
            arrived(1, 1, 1)
            send(3, 3, 0, 2, 1)
            send(1, 1, 1, 2, -1)
            send(2, 0, 1, 2, 1)
            send(2, 0, 0, 2, -1)
        if step == 3:
            arrived(0, 2, 0)
            arrived(0, 2, 1)
            share(0, 2)
            arrived(3, 3, 1)
            arrived(1, 1, 0)
            share(3, 3)
            share(1, 1)
        if step == 4:
            arrived(1, 3, 0)
            arrived(3, 1, 1)
            send(1, 3, 0, 2, 1)
            send(3, 1, 1, 2, -1)
            arrived(1, 3, 1)
            arrived(3, 1, 0)
            share(1, 3)
            share(3, 1)
        if step == 5:
            arrived(2, 3, 0)
            arrived(2, 1, 1)
            send(2, 3, 0, 2, 1)
            send(2, 1, 1, 2, -1)
            arrived(2, 3, 1)
            arrived(2, 1, 0)
            share(2, 3)
            share(2, 1)
        if step == 6:
            arrived(3, 2, 0)
            arrived(1, 2, 1)
            arrived(3, 2, 1)
            arrived(1, 2, 0)
            share(3, 2)
            share(1, 2)
        if step == 7:
            arrived(2, 2, 0)
            arrived(2, 2, 1)
            share(2, 2)

    first_of = [d1 for d1, _ in ORDER]
    second_of = [d2 for _, d2 in ORDER]

    def cotangents(u):
        d1, d2 = pick(first_of, u), pick(second_of, u)
        other = t2 * lax.rem(p2 + d1, SIDE) + t1 * lax.rem(p1 + d2, SIDE) + (1 - c)
        return [
            up[:, pl.ds(pl.multiple_of(dev * CHUNK, CHUNK), CHUNK)]
            for dev in (plane(d1, d2), other)
        ]

    def pair_step(step, carry):
        for i in range(PAIRS):
            @pl.when(step == i)
            def _(i=i):
                actions(i)

        for half in range(2):
            sib_copy(2 * step + half, half).wait_recv()
        cot = jnp.concatenate(cotangents(2 * step) + cotangents(2 * step + 1), axis=1).astype(F32)
        rows = slots[step]
        pre = lax.dot_general(w[...], rows, NT, preferred_element_type=F32)
        gate_pre, up_pre = pre[:HID], pre[HID:]
        sig = jax.nn.sigmoid(gate_pre)
        grad_gate = (cot * up_pre * (sig * (1.0 + gate_pre * (1.0 - sig)))).astype(BF16)
        grad_up = (cot * (gate_pre * sig)).astype(BF16)
        grads = jnp.concatenate([grad_gate, grad_up], axis=0)
        acc[...] += jnp.dot(grads, rows, preferred_element_type=F32)
        return carry

    lax.fori_loop(0, PAIRS, pair_step, 0)
    pending = []

    def go(copy):
        copy.start()
        pending.append(copy)
        return copy

    def drain():
        for i, (d1, d2, h) in enumerate(started):
            remote(
                piece(d1, d2, h), piece(d1, d2, h), ag_send.at[i], ag_recv.at[0, 0], sibling
            ).wait_send()
        for u in range(UNITS):
            sib_copy(u, u % 2).wait_send()
        for copy in pending:
            copy.wait_send()
        store_delta.wait()
        store_left.wait()

    store_left = pltpu.make_async_copy(full, left_out, out_sem.at[1])
    store_delta = pltpu.make_async_copy(acc, delta_out, out_sem.at[0])
    store_delta.start()

    def left_part(k, g, dst):
        cols = pl.ds(512 * g, 512)
        block = acc[pl.ds(pl.multiple_of(HID * k, 32), HID), cols]
        high = block.astype(BF16)
        low = (block - high.astype(F32)).astype(BF16)
        dsplit[k, pl.ds(0, HID), cols] = high
        dsplit[k, pl.ds(HID, HID), cols] = low
        both = jnp.dot(r2t[k], high, preferred_element_type=F32)
        part = both[:RANK] + both[RANK:]
        part = part + jnp.dot(r2t[k, pl.ds(0, RANK), :], low, preferred_element_type=F32)
        for i in range(4):
            dst[4 * g + i] = part[:, 128 * i : 128 * (i + 1)]

    swaps = []
    for g in range(4):
        left_part(1 - c, g, snd_sib)
        group = pl.ds(4 * g, 4)
        swaps.append(
            go(remote(snd_sib.at[group], rcv_sib.at[group], a_send.at[g], a_recv.at[g], sibling))
        )
    for g in range(4):
        left_part(c, g, mine)
    for swap in swaps:
        swap.wait_recv()

    near_last = (2, 1, 3)
    near_first = (1, 3, 2)

    def group_at(q):
        return pl.ds(4 * q, 4)

    firsts = {}
    for off in near_last:
        q = lax.rem(p1 + off, SIDE)
        mine[group_at(q)] += rcv_sib[group_at(q)]
        firsts[off] = go(remote(
            mine.at[group_at(q)], recv1.at[off - 1],
            b_send.at[off - 1], b_recv.at[off - 1], first_peer(off),
        ))
    total = mine[group_at(p1)] + rcv_sib[group_at(p1)]
    for off in near_first:
        firsts[off].wait_recv()
        total = total + recv1[off - 1]
    s1[...] = total

    seconds = {}
    for off in near_last:
        seconds[off] = go(remote(
            s1.at[lax.rem(p2 + off, SIDE)], recv2.at[off - 1],
            c_send.at[off - 1], c_recv.at[off - 1], second_peer(off),
        ))
    total = s1[p2]
    for off in near_first:
        seconds[off].wait_recv()
        total = total + recv2[off - 1]
    s2[...] = total

    far_first = (4, 3, 5, 2, 6, 1, 7)
    far_last = far_first[::-1]

    def eight(i):
        return pl.ds(pl.multiple_of(8 * i, 8), 8)

    reps = {}
    for off in far_first:
        reps[off] = go(remote(
            s2.at[eight(lax.rem(z + off, REPS)), :], recv3.at[off - 1],
            z_send.at[off - 1], z_recv.at[off - 1], rep_peer(off),
        ))
    total = s2[eight(z), :]
    for off in far_last:
        reps[off].wait_recv()
        total = total + recv3[off - 1]

    whole[eight(z), :] = total * (1.0 / REPS)
    reps = {}
    for off in far_first:
        reps[off] = go(remote(
            whole.at[eight(z), :], whole.at[eight(z), :],
            gz_send.at[off - 1], gz_recv.at[off - 1], rep_peer(off),
        ))
    for off in far_last:
        reps[off].wait_recv()

    own_block = full.at[c, 4 * p1 + p2]
    own_block[...] = whole[...].astype(BF16)
    seconds = {}
    for off in near_last:
        seconds[off] = go(remote(
            own_block, own_block, gb_send.at[off - 1], gb_recv.at[off - 1], second_peer(off)
        ))
    for off in near_first:
        seconds[off].wait_recv()

    def pass_on(off):
        group = full.at[c, group_at(lax.rem(p1 + SIDE - off, SIDE))]
        return go(remote(group, group, gs_send.at[off], gs_recv.at[off], sibling))

    own_group = full.at[c, group_at(p1)]
    firsts = {}
    for off in near_last:
        firsts[off] = go(remote(
            own_group, own_group, gc_send.at[off - 1], gc_recv.at[off - 1], first_peer(off)
        ))
    passed = [pass_on(0)]
    for off in near_first:
        firsts[off].wait_recv()
        passed.append(pass_on(off))

    lane = lax.broadcasted_iota(jnp.int32, (RANK, 128), 1)
    row = lax.broadcasted_iota(jnp.int32, (RANK, 128), 0)

    def left_rows(k):
        return jnp.concatenate([full[k, i] for i in range(16)], axis=1)

    def product(k):
        left = left_rows(k)
        twice = jnp.concatenate([left, left], axis=0)
        part = lax.dot_general(dsplit[k], twice, NT, preferred_element_type=F32)
        return part[:HID] + part[HID:]

    prod_own = product(c)
    for copy in passed:
        copy.wait_recv()
    prod_other = product(1 - c)
    wide = lax.broadcasted_iota(jnp.int32, (HID, 128), 1)
    psum[pl.ds(0, HID), :] = jnp.where((wide < RANK) == (c == 0), prod_own, prod_other)
    psum[pl.ds(HID, 32), :] = jnp.zeros((32, 128), F32)

    def p_rows(i):
        return pl.ds(pl.multiple_of(32 * i, 32), 32)

    reps = {}
    for off in far_first:
        reps[off] = go(remote(
            psum.at[p_rows(lax.rem(z + off, REPS)), :], recv4.at[off - 1],
            pz_send.at[off - 1], pz_recv.at[off - 1], rep_peer(off),
        ))
    store_left.start()

    for k in range(2):
        left = left_rows(k)
        padded = jnp.concatenate([left, jnp.zeros_like(left)], axis=0)
        gram = lax.dot_general(left, padded, NT, preferred_element_type=F32)
        aug[k] = jnp.where(lane == row + RANK, 1.0, gram)

    def eliminate(j, carry):
        for k in range(2):
            table = aug[k]
            pivot_row = aug[k, pl.ds(j, 1), :]
            at_j = lane == j
            pivot = jnp.sum(jnp.where(at_j[:1], pivot_row, 0.0), axis=1, keepdims=True)
            column = jnp.sum(jnp.where(at_j, table, 0.0), axis=1, keepdims=True)
            inv = lax.rsqrt(pivot)
            scaled = pivot_row * inv
            factor = column * inv
            aug[k] = jnp.where(
                row > j, table - factor * scaled, jnp.where(row == j, scaled, table)
            )
        return carry

    lax.fori_loop(0, RANK // 2, eliminate, 0)

    total = psum[p_rows(z), :]
    for off in far_last:
        reps[off].wait_recv()
        total = total + recv4[off - 1]
    pfull[p_rows(z), :] = total * (1.0 / REPS)
    reps = {}
    for off in far_first:
        reps[off] = go(remote(
            pfull.at[p_rows(z), :], pfull.at[p_rows(z), :],
            pg_send.at[off - 1], pg_recv.at[off - 1], rep_peer(off),
        ))

    lax.fori_loop(RANK // 2, RANK, eliminate, 0)

    inverse0 = jnp.where(lane < RANK, pltpu.roll(aug[0], RANK, 1), 0.0)
    inverse1 = jnp.where(lane >= RANK, aug[1], 0.0)
    solve_out[pl.ds(0, RANK), :] = inverse0
    solve_out[pl.ds(RANK, RANK), :] = inverse1
    both = jnp.concatenate([inverse0, inverse1], axis=0)
    solve_out[pl.ds(2 * RANK, 2 * RANK), :] = jnp.dot(
        both.T, both, precision=highest, preferred_element_type=F32
    )

    for off in far_last:
        reps[off].wait_recv()
    p_out[...] = pfull[...]

    drain()


AG_SENDS = 30


def step_call(tokens, upstream, weight, feedback, right_factor):
    any_space = pl.BlockSpec(memory_space=pl.ANY)
    vmem = pl.BlockSpec(memory_space=pltpu.VMEM)
    dma = pltpu.SemaphoreType.DMA
    return pl.pallas_call(
        step_kernel,
        name="gather_reduce",
        out_shape=(
            jax.ShapeDtypeStruct((2 * HID, DIM), F32),
            jax.ShapeDtypeStruct((2, 16, RANK, 128), BF16),
            jax.ShapeDtypeStruct((256, 128), F32),
            jax.ShapeDtypeStruct((256, 128), F32),
        ),
        in_specs=[any_space] * 5,
        out_specs=(any_space, any_space, vmem, vmem),
        scratch_shapes=[
            pltpu.VMEM((PAIRS, 4 * CHUNK, DIM), BF16),
            pltpu.VMEM((2 * HID, DIM), F32),
            pltpu.VMEM((2 * HID, DIM), BF16),
            pltpu.VMEM((HID, 32 * CHUNK), BF16),
            pltpu.VMEM((2, RANK, HID), F32),
            pltpu.VMEM((2, 2 * RANK, HID), BF16),
            pltpu.VMEM((2, 2 * HID, DIM), BF16),
            pltpu.VMEM((16, RANK, 128), F32),
            pltpu.VMEM((16, RANK, 128), F32),
            pltpu.VMEM((16, RANK, 128), F32),
            pltpu.VMEM((3, 4, RANK, 128), F32),
            pltpu.VMEM((4, RANK, 128), F32),
            pltpu.VMEM((3, RANK, 128), F32),
            pltpu.VMEM((RANK, 128), F32),
            pltpu.VMEM((7, 8, 128), F32),
            pltpu.VMEM((RANK, 128), F32),
            pltpu.VMEM((2, 16, RANK, 128), BF16),
            pltpu.VMEM((256, 128), F32),
            pltpu.VMEM((7, 32, 128), F32),
            pltpu.VMEM((256, 128), F32),
            pltpu.VMEM((2, RANK, 128), F32),
            dma((5,)), dma((2,)),
            dma((AG_SENDS,)), dma((UNITS, 2)), dma((UNITS,)), dma((UNITS,)),
            dma((4,)), dma((4,)), dma((3,)), dma((3,)), dma((3,)), dma((3,)), dma((7,)), dma((7,)),
            dma((7,)), dma((7,)), dma((3,)), dma((3,)), dma((3,)), dma((3,)), dma((4,)), dma((4,)),
            dma((7,)), dma((7,)), dma((7,)), dma((7,)),
        ],
        compiler_params=pltpu.CompilerParams(
            collective_id=0, has_side_effects=True, vmem_limit_bytes=60 * 1024 * 1024
        ),
    )(
        tokens.reshape(CHUNK, DIM),
        upstream.reshape(HID, 32 * CHUNK),
        weight.reshape(2 * HID, DIM),
        feedback.reshape(2 * HID, DIM),
        jnp.swapaxes(right_factor, 1, 2),
    )


COLS = 256


def finish_kernel(
    z_ref, delta, left, solve, p, momentum, weight, fb_out, mom_out, w_out, right_out, coef
):
    j = pl.program_id(0)

    @pl.when(j == 0)
    def _():
        rows = p[pl.ds(0, HID), :]
        right = lax.dot_general(
            solve[pl.ds(0, 2 * RANK), :], rows, NT, precision=highest, preferred_element_type=F32
        )
        right_out[0] = right[:RANK]
        right_out[1] = right[RANK:]
        weights = lax.dot_general(
            rows, solve[pl.ds(2 * RANK, 2 * RANK), :], NT,
            precision=highest, preferred_element_type=F32,
        )
        lane = lax.broadcasted_iota(jnp.int32, (HID, 128), 1)
        for k in range(2):
            own = jnp.where((lane < RANK) == (k == 0), weights, 0.0)
            high = own.astype(BF16)
            coef[pl.ds(2 * k * HID, HID), :] = high
            coef[pl.ds((2 * k + 1) * HID, HID), :] = (own - high.astype(F32)).astype(BF16)

    block = jnp.concatenate(
        [jnp.concatenate([left[k, i] for i in range(COLS // 128)], axis=1) for k in range(2)], axis=0
    )
    terms = jnp.dot(coef[...], block, preferred_element_type=F32)
    for k in range(2):
        approx = terms[2 * k * HID : (2 * k + 1) * HID] + terms[(2 * k + 1) * HID : 2 * (k + 1) * HID]
        fb_out[k] = delta[k] - approx

        @pl.when(j == z_ref[0])
        def _(k=k, approx=approx):
            moved = momentum_decay * momentum[k] + approx
            mom_out[k] = moved
            w_out[k] = (weight[k].astype(F32) - step_rate * moved).astype(BF16)


def finish_call(slab, delta, left, solve, p, momentum, weight):
    whole = lambda *shape: pl.BlockSpec(shape, lambda j, s: (0,) * len(shape))
    return pl.pallas_call(
        finish_kernel,
        name="finish",
        grid_spec=pltpu.PrefetchScalarGridSpec(
            num_scalar_prefetch=1,
            grid=(DIM // COLS,),
            in_specs=[
                pl.BlockSpec((2, HID, COLS), lambda j, s: (0, 0, j)),
                pl.BlockSpec((2, COLS // 128, RANK, 128), lambda j, s: (0, j, 0, 0)),
                whole(256, 128),
                whole(256, 128),
                whole(2, HID, COLS),
                pl.BlockSpec((2, HID, COLS), lambda j, s: (0, 0, s[0])),
            ],
            out_specs=[
                pl.BlockSpec((2, HID, COLS), lambda j, s: (0, 0, j)),
                whole(2, HID, COLS),
                whole(2, HID, COLS),
                whole(2, RANK, HID),
            ],
            scratch_shapes=[pltpu.VMEM((4 * HID, 2 * RANK), BF16)],
        ),
        out_shape=(
            jax.ShapeDtypeStruct((2, HID, DIM), F32),
            jax.ShapeDtypeStruct((2, HID, COLS), F32),
            jax.ShapeDtypeStruct((2, HID, COLS), BF16),
            jax.ShapeDtypeStruct((2, RANK, HID), F32),
        ),
        compiler_params=pltpu.CompilerParams(dimension_semantics=("arbitrary",)),
    )(slab, delta, left, solve, p, momentum, weight)


def per_device(tokens, upstream, weight, feedback, momentum, right_factor):
    delta, left, solve, p = step_call(tokens, upstream, weight, feedback, right_factor)
    slab = lax.axis_index("rep").astype(jnp.int32).reshape(1)
    feedback_next, momentum_next, weight_next, right_next = finish_call(
        slab, delta.reshape(2, HID, DIM), left, solve, p, momentum, weight
    )
    return (feedback_next[None], momentum_next, weight_next, jnp.swapaxes(right_next, 1, 2))


def solution(mesh):
    placed = (
        P("rep", "fsdp", None),
        P("rep", "fsdp", None),
        P(None, "fsdp", None),
        P("rep", None, "fsdp", None),
        P(None, "fsdp", "rep"),
        P(None, "fsdp", None),
    )
    return jax.shard_map(
        per_device,
        mesh=mesh,
        in_specs=placed,
        out_specs=(
            P("rep", None, "fsdp", None),
            P(None, "fsdp", "rep"),
            P(None, "fsdp", "rep"),
            P(None, "fsdp", None),
        ),
        check_vma=False,
    )
```

```python
import functools

import jax
import jax.numpy as jnp
from jax import lax
from jax.experimental import pallas as pl
from jax.experimental.pallas import tpu as pltpu
from jax.sharding import PartitionSpec as P

momentum_decay = 0.9
step_rate = 0.05
highest = lax.Precision.HIGHEST
MESH = pl.DeviceIdType.MESH
F32 = jnp.float32
BF16 = jnp.bfloat16

CHUNK = 128
HALF = 64
DIM = 2048
HID = 224
RANK = 64
REPS = 8
SIDE = 4
NT = (((1,), (1,)), ((), ()))

ORDER = [
    (0, 0), (3, 0),
    (1, 0), (0, 3),
    (0, 1), (2, 0),
    (0, 2), (3, 3),
    (1, 1), (1, 3),
    (3, 1), (2, 3),
    (2, 1), (3, 2),
    (1, 2), (2, 2),
]
UNIT = {pos: i for i, pos in enumerate(ORDER)}
UNITS = len(ORDER)
PAIRS = UNITS // 2


def pick(table, u):
    out = jnp.int32(0)
    for i, v in enumerate(table):
        if v:
            out = out + jnp.where(u == i, jnp.int32(v), jnp.int32(0))
    return out


def step_kernel(
    tok_hbm, up_hbm, w_hbm, fb_hbm, rf_hbm,
    delta_out, left_out, solve_out, p_out,
    slots, acc, w, up, rf, r2t, dsplit,
    snd_sib, rcv_sib, mine, recv1, s1, recv2, s2, recv3, whole, full, lsplit, psum, recv4, pfull,
    in_sem, out_sem, ag_send, ag_recv, sib_send, sib_recv,
    a_send, a_recv, b_send, b_recv, c_send, c_recv, z_send, z_recv,
    gz_send, gz_recv, gb_send, gb_recv, gc_send, gc_recv, gs_send, gs_recv,
    pz_send, pz_recv, pg_send, pg_recv,
):
    f = lax.axis_index("fsdp")
    z = lax.axis_index("rep")
    c = lax.rem(f, 2)
    x = lax.rem(lax.div(f, 2), SIDE)
    y = lax.div(f, 2 * SIDE)
    p1 = x * (1 - c) + y * c
    p2 = y * (1 - c) + x * c
    t1 = 2 + 6 * c
    t2 = 8 - 6 * c

    def plane(q1, q2):
        return t1 * lax.rem(p1 + q1, SIDE) + t2 * lax.rem(p2 + q2, SIDE) + c

    def first_peer(off):
        return (plane(off, 0), z)

    def second_peer(off):
        return (plane(0, off), z)

    def rep_peer(off):
        return (f, lax.rem(z + off, REPS))

    sibling = (f + 1 - 2 * c, z)

    def remote(src, dst, ssem, rsem, dev):
        return pltpu.make_async_remote_copy(
            src_ref=src, dst_ref=dst, send_sem=ssem, recv_sem=rsem,
            device_id=dev, device_id_type=MESH,
        )

    load_tok = pltpu.make_async_copy(tok_hbm, slots.at[0, pl.ds(0, CHUNK), :], in_sem.at[0])
    load_tok.start()
    loads = [
        pltpu.make_async_copy(w_hbm, w, in_sem.at[1]),
        pltpu.make_async_copy(up_hbm, up, in_sem.at[2]),
        pltpu.make_async_copy(fb_hbm, acc, in_sem.at[3]),
        pltpu.make_async_copy(rf_hbm, rf, in_sem.at[4]),
    ]
    for copy in loads:
        copy.start()

    barrier = pltpu.get_barrier_semaphore()
    peers = [sibling]
    peers += [first_peer(o) for o in (1, 2, 3)]
    peers += [second_peer(o) for o in (1, 2, 3)]
    peers += [rep_peer(o) for o in range(1, REPS)]
    for dev in peers:
        pl.semaphore_signal(barrier, inc=1, device_id=dev, device_id_type=MESH)
    load_tok.wait()
    pl.semaphore_wait(barrier, len(peers))

    started = []

    def piece(d1, d2, h):
        u = UNIT[(d1, d2)]
        return slots.at[u // 2, pl.ds(2 * CHUNK * (u % 2) + HALF * h, HALF), :]

    def send(d1, d2, h, axis, way):
        if axis == 1:
            r1, r2 = (d1 - way) % SIDE, d2
            dev = first_peer(way % SIDE)
        else:
            r1, r2 = d1, (d2 - way) % SIDE
            dev = second_peer(way % SIDE)
        copy = remote(
            piece(d1, d2, h), piece(r1, r2, h),
            ag_send.at[len(started)], ag_recv.at[UNIT[(r1, r2)], h], dev,
        )
        copy.start()
        started.append((d1, d2, h))

    def arrived(d1, d2, h):
        remote(
            piece(d1, d2, h), piece(d1, d2, h),
            ag_send.at[0], ag_recv.at[UNIT[(d1, d2)], h], sibling,
        ).wait_recv()

    def sib_copy(u, half):
        start = 2 * CHUNK * half
        pair = slots.at[lax.div(u, 2)]
        return remote(
            pair.at[pl.ds(start, CHUNK), :], pair.at[pl.ds(start + CHUNK, CHUNK), :],
            sib_send.at[u], sib_recv.at[u], sibling,
        )

    def share(d1, d2):
        u = UNIT[(d1, d2)]
        sib_copy(u, u % 2).start()

    send(0, 0, 0, 1, 1)
    send(0, 0, 1, 1, -1)
    share(0, 0)
    send(0, 0, 1, 1, 1)
    send(0, 0, 0, 1, -1)
    for copy in loads:
        copy.wait()

    for k in range(2):
        turned = rf[k]
        high = turned.astype(BF16)
        r2t[k, pl.ds(0, RANK), :] = high
        r2t[k, pl.ds(RANK, RANK), :] = (turned - high.astype(F32)).astype(BF16)

    def actions(step):
        if step == 0:
            arrived(3, 0, 0)
            arrived(1, 0, 1)
            send(3, 0, 0, 1, 1)
            send(1, 0, 1, 1, -1)
            send(0, 0, 0, 2, 1)
            send(0, 0, 1, 2, -1)
            send(0, 0, 1, 2, 1)
            send(0, 0, 0, 2, -1)
            send(3, 0, 0, 2, 1)
            send(1, 0, 1, 2, -1)
            send(1, 0, 1, 2, 1)
            send(3, 0, 0, 2, -1)
            arrived(3, 0, 1)
            arrived(1, 0, 0)
            share(3, 0)
            share(1, 0)
            send(3, 0, 1, 2, 1)
            send(1, 0, 0, 2, -1)
            send(1, 0, 0, 2, 1)
            send(3, 0, 1, 2, -1)
        if step == 1:
            arrived(0, 3, 0)
            arrived(0, 1, 1)
            send(0, 3, 0, 2, 1)
            send(0, 1, 1, 2, -1)
            arrived(0, 3, 1)
            arrived(0, 1, 0)
            share(0, 3)
            share(0, 1)
            arrived(2, 0, 0)
            arrived(2, 0, 1)
            send(2, 0, 0, 2, 1)
            send(2, 0, 1, 2, -1)
            share(2, 0)
        if step == 2:
            arrived(3, 3, 0)
            arrived(1, 1, 1)
            send(3, 3, 0, 2, 1)
            send(1, 1, 1, 2, -1)
            send(2, 0, 1, 2, 1)
            send(2, 0, 0, 2, -1)
        if step == 3:
            arrived(0, 2, 0)
            arrived(0, 2, 1)
            share(0, 2)
            arrived(3, 3, 1)
            arrived(1, 1, 0)
            share(3, 3)
            share(1, 1)
        if step == 4:
            arrived(1, 3, 0)
            arrived(3, 1, 1)
            send(1, 3, 0, 2, 1)
            send(3, 1, 1, 2, -1)
            arrived(1, 3, 1)
            arrived(3, 1, 0)
            share(1, 3)
            share(3, 1)
        if step == 5:
            arrived(2, 3, 0)
            arrived(2, 1, 1)
            send(2, 3, 0, 2, 1)
            send(2, 1, 1, 2, -1)
            arrived(2, 3, 1)
            arrived(2, 1, 0)
            share(2, 3)
            share(2, 1)
        if step == 6:
            arrived(3, 2, 0)
            arrived(1, 2, 1)
            arrived(3, 2, 1)
            arrived(1, 2, 0)
            share(3, 2)
            share(1, 2)
        if step == 7:
            arrived(2, 2, 0)
            arrived(2, 2, 1)
            share(2, 2)

    first_of = [d1 for d1, _ in ORDER]
    second_of = [d2 for _, d2 in ORDER]

    def cotangents(u):
        d1, d2 = pick(first_of, u), pick(second_of, u)
        other = t2 * lax.rem(p2 + d1, SIDE) + t1 * lax.rem(p1 + d2, SIDE) + (1 - c)
        return [
            up[:, pl.ds(pl.multiple_of(dev * CHUNK, CHUNK), CHUNK)]
            for dev in (plane(d1, d2), other)
        ]

    def pair_step(step, carry):
        for i in range(PAIRS):
            @pl.when(step == i)
            def _(i=i):
                actions(i)

        for half in range(2):
            sib_copy(2 * step + half, half).wait_recv()
        cot = jnp.concatenate(cotangents(2 * step) + cotangents(2 * step + 1), axis=1).astype(F32)
        rows = slots[step]
        pre = lax.dot_general(w[...], rows, NT, preferred_element_type=F32)
        gate_pre, up_pre = pre[:HID], pre[HID:]
        sig = jax.nn.sigmoid(gate_pre)
        grad_gate = (cot * up_pre * (sig * (1.0 + gate_pre * (1.0 - sig)))).astype(BF16)
        grad_up = (cot * (gate_pre * sig)).astype(BF16)
        grads = jnp.concatenate([grad_gate, grad_up], axis=0)
        acc[...] += jnp.dot(grads, rows, preferred_element_type=F32)
        return carry

    lax.fori_loop(0, PAIRS, pair_step, 0)
    pending = []

    def go(copy):
        copy.start()
        pending.append(copy)
        return copy

    def drain():
        for i, (d1, d2, h) in enumerate(started):
            remote(
                piece(d1, d2, h), piece(d1, d2, h), ag_send.at[i], ag_recv.at[0, 0], sibling
            ).wait_send()
        for u in range(UNITS):
            sib_copy(u, u % 2).wait_send()
        for copy in pending:
            copy.wait_send()
        store_delta.wait()
        store_left.wait()

    store_left = pltpu.make_async_copy(lsplit, left_out, out_sem.at[1])
    store_delta = pltpu.make_async_copy(acc, delta_out, out_sem.at[0])
    store_delta.start()

    def left_part(k, g, dst):
        cols = pl.ds(512 * g, 512)
        block = acc[pl.ds(pl.multiple_of(HID * k, 32), HID), cols]
        high = block.astype(BF16)
        low = (block - high.astype(F32)).astype(BF16)
        dsplit[k, pl.ds(0, HID), cols] = high
        dsplit[k, pl.ds(HID, HID), cols] = low
        both = jnp.dot(r2t[k], high, preferred_element_type=F32)
        part = both[:RANK] + both[RANK:]
        part = part + jnp.dot(r2t[k, pl.ds(0, RANK), :], low, preferred_element_type=F32)
        for i in range(4):
            dst[4 * g + i] = part[:, 128 * i : 128 * (i + 1)]

    swaps = []
    for g in range(4):
        left_part(1 - c, g, snd_sib)
        group = pl.ds(4 * g, 4)
        swaps.append(
            go(remote(snd_sib.at[group], rcv_sib.at[group], a_send.at[g], a_recv.at[g], sibling))
        )
    for g in range(4):
        left_part(c, g, mine)
    for swap in swaps:
        swap.wait_recv()

    near_last = (2, 1, 3)
    near_first = (1, 3, 2)
    after, before = first_peer(1), first_peer(3)

    def group_of(off, half):
        return pl.ds(4 * lax.rem(p1 + off, SIDE) + 2 * half, 2)

    def add_sibling(off):
        group = pl.ds(4 * lax.rem(p1 + off, SIDE), 4)
        mine[group] += rcv_sib[group]

    def ring(group, slot, dev):
        return go(remote(mine.at[group], recv1.at[slot], b_send.at[slot], b_recv.at[slot], dev))

    add_sibling(2)
    hops = [ring(group_of(2, 0), 0, after), ring(group_of(2, 1), 3, before)]
    add_sibling(1)
    hops.append(ring(group_of(1, 1), 1, after))
    add_sibling(3)
    hops.append(ring(group_of(3, 0), 4, before))
    add_sibling(0)
    hops[0].wait_recv()
    mine[group_of(1, 0)] += recv1[0]
    hops.append(ring(group_of(1, 0), 2, after))
    hops[1].wait_recv()
    mine[group_of(3, 1)] += recv1[3]
    hops.append(ring(group_of(3, 1), 5, before))
    for hop in hops[2:]:
        hop.wait_recv()
    s1[pl.ds(0, 2)] = mine[group_of(0, 0)] + recv1[2] + recv1[4]
    s1[pl.ds(2, 2)] = mine[group_of(0, 1)] + recv1[1] + recv1[5]

    seconds = {}
    for off in near_last:
        seconds[off] = go(remote(
            s1.at[lax.rem(p2 + off, SIDE)], recv2.at[off - 1],
            c_send.at[off - 1], c_recv.at[off - 1], second_peer(off),
        ))
    total = s1[p2]
    for off in near_first:
        seconds[off].wait_recv()
        total = total + recv2[off - 1]
    s2[...] = total

    far_first = (4, 3, 5, 2, 6, 1, 7)
    far_last = far_first[::-1]

    def eight(i):
        return pl.ds(pl.multiple_of(8 * i, 8), 8)

    reps = {}
    for off in far_first:
        reps[off] = go(remote(
            s2.at[eight(lax.rem(z + off, REPS)), :], recv3.at[off - 1],
            z_send.at[off - 1], z_recv.at[off - 1], rep_peer(off),
        ))
    total = s2[eight(z), :]
    for off in far_last:
        reps[off].wait_recv()
        total = total + recv3[off - 1]

    whole[eight(z), :] = total * (1.0 / REPS)
    reps = {}
    for off in far_first:
        reps[off] = go(remote(
            whole.at[eight(z), :], whole.at[eight(z), :],
            gz_send.at[off - 1], gz_recv.at[off - 1], rep_peer(off),
        ))
    for off in far_last:
        reps[off].wait_recv()

    own_block = full.at[c, 4 * p1 + p2]
    own_block[...] = whole[...]
    seconds = {}
    for off in near_last:
        seconds[off] = go(remote(
            own_block, own_block, gb_send.at[off - 1], gb_recv.at[off - 1], second_peer(off)
        ))
    for off in near_first:
        seconds[off].wait_recv()

    def spread(off, half, slot, dev):
        group = full.at[c, group_of(off, half)]
        return go(remote(group, group, gc_send.at[slot], gc_recv.at[slot], dev))

    passed = []

    def pass_on(off, half):
        group = full.at[c, group_of(off, half)]
        n = len(passed)
        passed.append(go(remote(group, group, gs_send.at[n], gs_recv.at[n], sibling)))

    hops = [
        spread(0, 0, 0, after), spread(0, 1, 1, before),
        spread(0, 1, 2, after), spread(0, 0, 3, before),
    ]
    pass_on(0, 0)
    pass_on(0, 1)
    hops[0].wait_recv()
    hops.append(spread(3, 0, 4, after))
    hops[1].wait_recv()
    hops.append(spread(1, 1, 5, before))
    pass_on(3, 0)
    pass_on(1, 1)
    hops[2].wait_recv()
    pass_on(3, 1)
    hops[3].wait_recv()
    pass_on(1, 0)
    hops[4].wait_recv()
    pass_on(2, 0)
    hops[5].wait_recv()
    pass_on(2, 1)

    lane = lax.broadcasted_iota(jnp.int32, (RANK, 128), 1)
    row = lax.broadcasted_iota(jnp.int32, (RANK, 128), 0)

    def split_left(k):
        left = jnp.concatenate([full[k, i] for i in range(16)], axis=1)
        high = left.astype(BF16)
        rows = pl.ds(pl.multiple_of(RANK * k, RANK), RANK)
        lsplit[0, rows, :] = high
        lsplit[1, rows, :] = (left - high.astype(F32)).astype(BF16)

    def left_terms(k):
        rows = pl.ds(pl.multiple_of(RANK * k, RANK), RANK)
        return jnp.concatenate([lsplit[0, rows, :], lsplit[1, rows, :]], axis=0)

    def product(k):
        part = lax.dot_general(dsplit[k], left_terms(k), NT, preferred_element_type=F32)
        part = part[:HID] + part[HID:]
        part = part + pltpu.roll(part, RANK, 1)
        wide = lax.broadcasted_iota(jnp.int32, (HID // 2, 128), 1)
        return jnp.where(wide < RANK, part[: HID // 2], part[HID // 2 :])

    def p_rows(i):
        return pl.ds(pl.multiple_of(16 * i, 16), 16)

    def scatter(slot, k):
        psum[slot, pl.ds(0, HID // 2), :] = product(k)
        psum[slot, pl.ds(HID // 2, 16), :] = jnp.zeros((16, 128), F32)
        out = {}
        for off in far_first:
            n = 7 * slot + off - 1
            out[off] = go(remote(
                psum.at[slot, p_rows(lax.rem(z + off, REPS)), :], recv4.at[slot, off - 1],
                pz_send.at[n], pz_recv.at[n], rep_peer(off),
            ))
        return out

    split_left(c)
    parts = [scatter(0, c)]
    for copy in passed:
        copy.wait_recv()
    split_left(1 - c)
    parts.append(scatter(1, 1 - c))
    store_left.start()

    tables = []
    for k in range(2):
        terms = left_terms(k)
        gram = lax.dot_general(terms, terms, NT, preferred_element_type=F32)
        gram = gram[:RANK] + gram[RANK:]
        gram = gram + pltpu.roll(gram, RANK, 1)
        tables.append(jnp.where(lane < RANK, gram, jnp.where(lane == row + RANK, 1.0, 0.0)))

    def eliminate(j):
        for k in range(2):
            table = tables[k]
            inv = lax.rsqrt(table[j : j + 1, j : j + 1])
            scaled = table[j : j + 1, :] * inv
            factor = jnp.where(row[:, :1] > j, table[:, j : j + 1] * inv, 0.0)
            tables[k] = jnp.where(row == j, scaled, table - factor * scaled)

    for j in range(RANK // 2):
        eliminate(j)

    for slot in range(2):
        total = psum[slot, p_rows(z), :]
        for off in far_last:
            parts[slot][off].wait_recv()
            total = total + recv4[slot, off - 1]
        pfull[slot, p_rows(z), :] = total * (1.0 / REPS)
    reps = {}
    for off in far_first:
        reps[off] = go(remote(
            pfull.at[:, p_rows(z), :], pfull.at[:, p_rows(z), :],
            pg_send.at[off - 1], pg_recv.at[off - 1], rep_peer(off),
        ))

    for j in range(RANK // 2, RANK):
        eliminate(j)

    inverse0 = jnp.where(lane < RANK, pltpu.roll(tables[0], RANK, 1), 0.0)
    inverse1 = jnp.where(lane >= RANK, tables[1], 0.0)
    solve_out[pl.ds(0, RANK), :] = inverse0
    solve_out[pl.ds(RANK, RANK), :] = inverse1
    both = jnp.concatenate([inverse0, inverse1], axis=0)
    solve_out[pl.ds(2 * RANK, 2 * RANK), :] = jnp.dot(
        both.T, both, precision=highest, preferred_element_type=F32
    )

    for off in far_last:
        reps[off].wait_recv()
    own, other = pfull[0, pl.ds(0, HID // 2), :], pfull[1, pl.ds(0, HID // 2), :]
    gate = jnp.where(c == 0, own, other)
    gate = jnp.concatenate([gate, pltpu.roll(gate, RANK, 1)], axis=0)
    raised = jnp.where(c == 0, other, own)
    raised = jnp.concatenate([pltpu.roll(raised, RANK, 1), raised], axis=0)
    wide = lax.broadcasted_iota(jnp.int32, (HID, 128), 1)
    p_out[...] = jnp.where(wide < RANK, gate, raised)

    drain()


AG_SENDS = 30


def step_call(tokens, upstream, weight, feedback, right_factor):
    any_space = pl.BlockSpec(memory_space=pl.ANY)
    vmem = pl.BlockSpec(memory_space=pltpu.VMEM)
    dma = pltpu.SemaphoreType.DMA
    return pl.pallas_call(
        step_kernel,
        name="gather_reduce",
        out_shape=(
            jax.ShapeDtypeStruct((2 * HID, DIM), F32),
            jax.ShapeDtypeStruct((2, 2 * RANK, DIM), BF16),
            jax.ShapeDtypeStruct((256, 128), F32),
            jax.ShapeDtypeStruct((HID, 128), F32),
        ),
        in_specs=[any_space] * 5,
        out_specs=(any_space, any_space, vmem, vmem),
        scratch_shapes=[
            pltpu.VMEM((PAIRS, 4 * CHUNK, DIM), BF16),
            pltpu.VMEM((2 * HID, DIM), F32),
            pltpu.VMEM((2 * HID, DIM), BF16),
            pltpu.VMEM((HID, 32 * CHUNK), BF16),
            pltpu.VMEM((2, RANK, HID), F32),
            pltpu.VMEM((2, 2 * RANK, HID), BF16),
            pltpu.VMEM((2, 2 * HID, DIM), BF16),
            pltpu.VMEM((16, RANK, 128), F32),
            pltpu.VMEM((16, RANK, 128), F32),
            pltpu.VMEM((16, RANK, 128), F32),
            pltpu.VMEM((6, 2, RANK, 128), F32),
            pltpu.VMEM((4, RANK, 128), F32),
            pltpu.VMEM((3, RANK, 128), F32),
            pltpu.VMEM((RANK, 128), F32),
            pltpu.VMEM((7, 8, 128), F32),
            pltpu.VMEM((RANK, 128), F32),
            pltpu.VMEM((2, 16, RANK, 128), F32),
            pltpu.VMEM((2, 2 * RANK, DIM), BF16),
            pltpu.VMEM((2, 128, 128), F32),
            pltpu.VMEM((2, 7, 16, 128), F32),
            pltpu.VMEM((2, 128, 128), F32),
            dma((5,)), dma((2,)),
            dma((AG_SENDS,)), dma((UNITS, 2)), dma((UNITS,)), dma((UNITS,)),
            dma((4,)), dma((4,)), dma((6,)), dma((6,)), dma((3,)), dma((3,)), dma((7,)), dma((7,)),
            dma((7,)), dma((7,)), dma((3,)), dma((3,)), dma((6,)), dma((6,)), dma((8,)), dma((8,)),
            dma((14,)), dma((14,)), dma((7,)), dma((7,)),
        ],
        compiler_params=pltpu.CompilerParams(
            collective_id=0, has_side_effects=True, vmem_limit_bytes=60 * 1024 * 1024
        ),
    )(
        tokens.reshape(CHUNK, DIM),
        upstream.reshape(HID, 32 * CHUNK),
        weight.reshape(2 * HID, DIM),
        feedback.reshape(2 * HID, DIM),
        jnp.swapaxes(right_factor, 1, 2),
    )


COLS = 512
SLAB = DIM // REPS


def finish_kernel(
    delta_hbm, left_hbm, solve_hbm, p_hbm, mom_hbm, w_hbm, fb_out, mom_out, w_out, right_out,
    delta, left, solve, p, mom, w, wnext, right, coef, in_sem, out_sem,
):
    z = lax.axis_index("rep")
    slab = pl.ds(pl.multiple_of(SLAB * z, SLAB), SLAB)
    loads = [
        pltpu.make_async_copy(solve_hbm, solve, in_sem.at[0]),
        pltpu.make_async_copy(p_hbm, p, in_sem.at[1]),
        pltpu.make_async_copy(left_hbm, left, in_sem.at[2]),
    ]
    chunks = [pl.ds(COLS * j, COLS) for j in range(DIM // COLS)]
    for j, cols in enumerate(chunks):
        loads.append(
            pltpu.make_async_copy(delta_hbm.at[:, :, cols], delta.at[:, :, cols], in_sem.at[3 + j])
        )
    late = 3 + len(chunks)
    loads.append(pltpu.make_async_copy(mom_hbm, mom, in_sem.at[late]))
    loads.append(pltpu.make_async_copy(w_hbm.at[:, :, slab], w, in_sem.at[late + 1]))
    for copy in loads:
        copy.start()
    loads[0].wait()
    loads[1].wait()

    rows = p[...]
    weights = lax.dot_general(
        rows, solve[pl.ds(2 * RANK, 2 * RANK), :], NT,
        precision=highest, preferred_element_type=F32,
    )
    lane = lax.broadcasted_iota(jnp.int32, (HID, 128), 1)
    for k in range(2):
        own = jnp.where((lane < RANK) == (k == 0), weights, 0.0)
        high = own.astype(BF16)
        coef[pl.ds(k * HID, HID), :] = high
        coef[pl.ds((2 + k) * HID, HID), :] = (own - high.astype(F32)).astype(BF16)
    loads[2].wait()

    def approx_at(cols):
        terms = jnp.dot(coef[...], left[0, :, cols], preferred_element_type=F32)
        more = jnp.dot(coef[pl.ds(0, 2 * HID), :], left[1, :, cols], preferred_element_type=F32)
        return terms[: 2 * HID] + terms[2 * HID :] + more

    stores = []
    for j, cols in enumerate(chunks):
        approx = approx_at(cols)
        loads[3 + j].wait()
        for k in range(2):
            delta[k, :, cols] = delta[k, :, cols] - approx[k * HID : (k + 1) * HID]
        stores.append(
            pltpu.make_async_copy(delta.at[:, :, cols], fb_out.at[:, :, cols], out_sem.at[j])
        )
        stores[-1].start()

    approx = approx_at(slab)
    loads[late].wait()
    loads[late + 1].wait()
    for k in range(2):
        moved = momentum_decay * mom[k] + approx[k * HID : (k + 1) * HID]
        mom[k] = moved
        wnext[k] = (w[k].astype(F32) - step_rate * moved).astype(BF16)
    turned = lax.dot_general(
        solve[pl.ds(0, 2 * RANK), :], rows, NT, precision=highest, preferred_element_type=F32
    )
    right[0] = turned[:RANK]
    right[1] = turned[RANK:]
    n = len(chunks)
    stores.append(pltpu.make_async_copy(mom, mom_out, out_sem.at[n]))
    stores.append(pltpu.make_async_copy(wnext, w_out, out_sem.at[n + 1]))
    stores.append(pltpu.make_async_copy(right, right_out, out_sem.at[n + 2]))
    for copy in stores[n:]:
        copy.start()
    for copy in stores:
        copy.wait()


def finish_call(delta, left, solve, p, momentum, weight):
    any_space = pl.BlockSpec(memory_space=pl.ANY)
    dma = pltpu.SemaphoreType.DMA
    n = DIM // COLS
    return pl.pallas_call(
        finish_kernel,
        name="finish",
        in_specs=[any_space] * 6,
        out_specs=(any_space,) * 4,
        out_shape=(
            jax.ShapeDtypeStruct((2, HID, DIM), F32),
            jax.ShapeDtypeStruct((2, HID, SLAB), F32),
            jax.ShapeDtypeStruct((2, HID, SLAB), BF16),
            jax.ShapeDtypeStruct((2, RANK, HID), F32),
        ),
        scratch_shapes=[
            pltpu.VMEM((2, HID, DIM), F32),
            pltpu.VMEM((2, 2 * RANK, DIM), BF16),
            pltpu.VMEM((256, 128), F32),
            pltpu.VMEM((HID, 128), F32),
            pltpu.VMEM((2, HID, SLAB), F32),
            pltpu.VMEM((2, HID, SLAB), BF16),
            pltpu.VMEM((2, HID, SLAB), BF16),
            pltpu.VMEM((2, RANK, HID), F32),
            pltpu.VMEM((4 * HID, 2 * RANK), BF16),
            dma((n + 5,)), dma((n + 3,)),
        ],
        compiler_params=pltpu.CompilerParams(vmem_limit_bytes=32 * 1024 * 1024),
    )(delta, left, solve, p, momentum, weight)


def per_device(tokens, upstream, weight, feedback, momentum, right_factor):
    delta, left, solve, p = step_call(tokens, upstream, weight, feedback, right_factor)
    feedback_next, momentum_next, weight_next, right_next = finish_call(
        delta.reshape(2, HID, DIM), left, solve, p, momentum, weight
    )
    return (feedback_next[None], momentum_next, weight_next, jnp.swapaxes(right_next, 1, 2))


def solution(mesh):
    placed = (
        P("rep", "fsdp", None),
        P("rep", "fsdp", None),
        P(None, "fsdp", None),
        P("rep", None, "fsdp", None),
        P(None, "fsdp", "rep"),
        P(None, "fsdp", None),
    )
    return jax.shard_map(
        per_device,
        mesh=mesh,
        in_specs=placed,
        out_specs=(
            P("rep", None, "fsdp", None),
            P(None, "fsdp", "rep"),
            P(None, "fsdp", "rep"),
            P(None, "fsdp", None),
        ),
        check_vma=False,
    )
```

```python
import functools

import jax
import jax.numpy as jnp
from jax import lax
from jax.experimental import pallas as pl
from jax.experimental.pallas import tpu as pltpu
from jax.sharding import PartitionSpec as P

momentum_decay = 0.9
step_rate = 0.05
highest = lax.Precision.HIGHEST
MESH = pl.DeviceIdType.MESH
F32 = jnp.float32
BF16 = jnp.bfloat16

CHUNK = 128
HALF = 64
DIM = 2048
HID = 224
RANK = 64
REPS = 8
SIDE = 4
NT = (((1,), (1,)), ((), ()))

ORDER = [
    (0, 0), (3, 0),
    (1, 0), (0, 3),
    (0, 1), (2, 0),
    (0, 2), (3, 3),
    (1, 1), (1, 3),
    (3, 1), (2, 3),
    (2, 1), (3, 2),
    (1, 2), (2, 2),
]
UNIT = {pos: i for i, pos in enumerate(ORDER)}
UNITS = len(ORDER)
PAIRS = UNITS // 2


def pick(table, u):
    out = jnp.int32(0)
    for i, v in enumerate(table):
        if v:
            out = out + jnp.where(u == i, jnp.int32(v), jnp.int32(0))
    return out


def step_kernel(
    tok_hbm, up_hbm, w_hbm, fb_hbm, rf_hbm,
    delta_out, left_out, solve_out, p_out,
    slots, acc, w, up, rf, r2t, dsplit,
    snd_sib, rcv_sib, mine, recv1, s1, recv2, s2, recv3, whole, full, lsplit, psum, recv4, pfull,
    in_sem, out_sem, ag_send, ag_recv, sib_send, sib_recv,
    a_send, a_recv, b_send, b_recv, c_send, c_recv, z_send, z_recv,
    gz_send, gz_recv, gb_send, gb_recv, gc_send, gc_recv, gs_send, gs_recv,
    pz_send, pz_recv, pg_send, pg_recv, meet_sem,
):
    f = lax.axis_index("fsdp")
    z = lax.axis_index("rep")
    c = lax.rem(f, 2)
    x = lax.rem(lax.div(f, 2), SIDE)
    y = lax.div(f, 2 * SIDE)
    p1 = x * (1 - c) + y * c
    p2 = y * (1 - c) + x * c
    t1 = 2 + 6 * c
    t2 = 8 - 6 * c

    def plane(q1, q2):
        return t1 * lax.rem(p1 + q1, SIDE) + t2 * lax.rem(p2 + q2, SIDE) + c

    def first_peer(off):
        return (plane(off, 0), z)

    def second_peer(off):
        return (plane(0, off), z)

    def rep_peer(off):
        return (f, lax.rem(z + off, REPS))

    sibling = (f + 1 - 2 * c, z)

    def remote(src, dst, ssem, rsem, dev):
        return pltpu.make_async_remote_copy(
            src_ref=src, dst_ref=dst, send_sem=ssem, recv_sem=rsem,
            device_id=dev, device_id_type=MESH,
        )

    load_tok = pltpu.make_async_copy(tok_hbm, slots.at[0, pl.ds(0, CHUNK), :], in_sem.at[0])
    load_tok.start()
    loads = [
        pltpu.make_async_copy(w_hbm, w, in_sem.at[1]),
        pltpu.make_async_copy(up_hbm, up, in_sem.at[2]),
        pltpu.make_async_copy(fb_hbm, acc, in_sem.at[3]),
        pltpu.make_async_copy(rf_hbm, rf, in_sem.at[4]),
    ]
    for copy in loads:
        copy.start()

    barrier = pltpu.get_barrier_semaphore()
    peers = [sibling, first_peer(1), first_peer(3), second_peer(1), second_peer(3)]
    peers += [rep_peer(1), rep_peer(REPS - 1)]

    def meet(turn, off):
        for way in (off, REPS - off):
            pl.semaphore_signal(
                meet_sem.at[turn], inc=1, device_id=rep_peer(way), device_id_type=MESH
            )

    for dev in peers:
        pl.semaphore_signal(barrier, inc=1, device_id=dev, device_id_type=MESH)
    pl.semaphore_wait(barrier, len(peers))
    meet(0, 1)

    started = []

    def piece(d1, d2, h):
        u = UNIT[(d1, d2)]
        return slots.at[u // 2, pl.ds(2 * CHUNK * (u % 2) + HALF * h, HALF), :]

    def send(d1, d2, h, axis, way):
        if axis == 1:
            r1, r2 = (d1 - way) % SIDE, d2
            dev = first_peer(way % SIDE)
        else:
            r1, r2 = d1, (d2 - way) % SIDE
            dev = second_peer(way % SIDE)
        own = d1 == 0 and d2 == 0
        copy = remote(
            tok_hbm.at[pl.ds(HALF * h, HALF), :] if own else piece(d1, d2, h), piece(r1, r2, h),
            ag_send.at[len(started)], ag_recv.at[UNIT[(r1, r2)], h], dev,
        )
        copy.start()
        started.append((d1, d2, h))

    def arrived(d1, d2, h):
        remote(
            piece(d1, d2, h), piece(d1, d2, h),
            ag_send.at[0], ag_recv.at[UNIT[(d1, d2)], h], sibling,
        ).wait_recv()

    def sib_copy(u, half):
        start = 2 * CHUNK * half
        pair = slots.at[lax.div(u, 2)]
        return remote(
            pair.at[pl.ds(start, CHUNK), :], pair.at[pl.ds(start + CHUNK, CHUNK), :],
            sib_send.at[u], sib_recv.at[u], sibling,
        )

    def share(d1, d2):
        u = UNIT[(d1, d2)]
        sib_copy(u, u % 2).start()

    def share_own():
        remote(
            tok_hbm, slots.at[0, pl.ds(CHUNK, CHUNK), :], sib_send.at[0], sib_recv.at[0], sibling
        ).start()

    send(0, 0, 0, 1, 1)
    send(0, 0, 1, 1, -1)
    share_own()
    send(0, 0, 1, 1, 1)
    send(0, 0, 0, 1, -1)
    load_tok.wait()
    for copy in loads:
        copy.wait()

    for k in range(2):
        turned = rf[k]
        high = turned.astype(BF16)
        r2t[k, pl.ds(0, RANK), :] = high
        r2t[k, pl.ds(RANK, RANK), :] = (turned - high.astype(F32)).astype(BF16)

    def actions(step):
        if step == 0:
            arrived(3, 0, 0)
            arrived(1, 0, 1)
            send(3, 0, 0, 1, 1)
            send(1, 0, 1, 1, -1)
            send(0, 0, 0, 2, 1)
            send(0, 0, 1, 2, -1)
            send(0, 0, 1, 2, 1)
            send(0, 0, 0, 2, -1)
            send(3, 0, 0, 2, 1)
            send(1, 0, 1, 2, -1)
            send(1, 0, 1, 2, 1)
            send(3, 0, 0, 2, -1)
            arrived(3, 0, 1)
            arrived(1, 0, 0)
            share(3, 0)
            share(1, 0)
            send(3, 0, 1, 2, 1)
            send(1, 0, 0, 2, -1)
            send(1, 0, 0, 2, 1)
            send(3, 0, 1, 2, -1)
        if step == 1:
            arrived(0, 3, 0)
            arrived(0, 1, 1)
            send(0, 3, 0, 2, 1)
            send(0, 1, 1, 2, -1)
            arrived(0, 3, 1)
            arrived(0, 1, 0)
            share(0, 3)
            share(0, 1)
            arrived(2, 0, 0)
            arrived(2, 0, 1)
            send(2, 0, 0, 2, 1)
            send(2, 0, 1, 2, -1)
            share(2, 0)
        if step == 2:
            arrived(3, 3, 0)
            arrived(1, 1, 1)
            send(3, 3, 0, 2, 1)
            send(1, 1, 1, 2, -1)
            send(2, 0, 1, 2, 1)
            send(2, 0, 0, 2, -1)
            pl.semaphore_wait(meet_sem.at[0], 2)
            meet(1, 2)
        if step == 3:
            arrived(0, 2, 0)
            arrived(0, 2, 1)
            share(0, 2)
            arrived(3, 3, 1)
            arrived(1, 1, 0)
            share(3, 3)
            share(1, 1)
        if step == 4:
            arrived(1, 3, 0)
            arrived(3, 1, 1)
            send(1, 3, 0, 2, 1)
            send(3, 1, 1, 2, -1)
            arrived(1, 3, 1)
            arrived(3, 1, 0)
            share(1, 3)
            share(3, 1)
        if step == 5:
            arrived(2, 3, 0)
            arrived(2, 1, 1)
            send(2, 3, 0, 2, 1)
            send(2, 1, 1, 2, -1)
            arrived(2, 3, 1)
            arrived(2, 1, 0)
            share(2, 3)
            share(2, 1)
            pl.semaphore_wait(meet_sem.at[1], 2)
        if step == 6:
            arrived(3, 2, 0)
            arrived(1, 2, 1)
            arrived(3, 2, 1)
            arrived(1, 2, 0)
            share(3, 2)
            share(1, 2)
        if step == 7:
            arrived(2, 2, 0)
            arrived(2, 2, 1)
            share(2, 2)

    first_of = [d1 for d1, _ in ORDER]
    second_of = [d2 for _, d2 in ORDER]

    def cotangents(u):
        d1, d2 = pick(first_of, u), pick(second_of, u)
        other = t2 * lax.rem(p2 + d1, SIDE) + t1 * lax.rem(p1 + d2, SIDE) + (1 - c)
        return [
            up[:, pl.ds(pl.multiple_of(dev * CHUNK, CHUNK), CHUNK)]
            for dev in (plane(d1, d2), other)
        ]

    def pair_step(step, carry):
        for i in range(PAIRS):
            @pl.when(step == i)
            def _(i=i):
                actions(i)

        for half in range(2):
            sib_copy(2 * step + half, half).wait_recv()
        cot = jnp.concatenate(cotangents(2 * step) + cotangents(2 * step + 1), axis=1).astype(F32)
        rows = slots[step]
        pre = lax.dot_general(w[...], rows, NT, preferred_element_type=F32)
        gate_pre, up_pre = pre[:HID], pre[HID:]
        sig = jax.nn.sigmoid(gate_pre)
        grad_gate = (cot * up_pre * (sig * (1.0 + gate_pre * (1.0 - sig)))).astype(BF16)
        grad_up = (cot * (gate_pre * sig)).astype(BF16)
        grads = jnp.concatenate([grad_gate, grad_up], axis=0)
        acc[...] += jnp.dot(grads, rows, preferred_element_type=F32)
        return carry

    lax.fori_loop(0, PAIRS, pair_step, 0)
    pending = []

    def go(copy):
        copy.start()
        pending.append(copy)
        return copy

    def drain():
        for i, (d1, d2, h) in enumerate(started):
            remote(
                piece(d1, d2, h), piece(d1, d2, h), ag_send.at[i], ag_recv.at[0, 0], sibling
            ).wait_send()
        for u in range(UNITS):
            sib_copy(u, u % 2).wait_send()
        for copy in pending:
            copy.wait_send()
        store_delta.wait()
        store_left.wait()

    store_left = pltpu.make_async_copy(lsplit, left_out, out_sem.at[1])
    store_delta = pltpu.make_async_copy(acc, delta_out, out_sem.at[0])
    store_delta.start()

    def left_part(k, g, dst):
        cols = pl.ds(512 * g, 512)
        block = acc[pl.ds(pl.multiple_of(HID * k, 32), HID), cols]
        high = block.astype(BF16)
        low = (block - high.astype(F32)).astype(BF16)
        dsplit[k, pl.ds(0, HID), cols] = high
        dsplit[k, pl.ds(HID, HID), cols] = low
        both = jnp.dot(r2t[k], high, preferred_element_type=F32)
        part = both[:RANK] + both[RANK:]
        part = part + jnp.dot(r2t[k, pl.ds(0, RANK), :], low, preferred_element_type=F32)
        for i in range(4):
            dst[4 * g + i] = part[:, 128 * i : 128 * (i + 1)]

    swaps = []
    for g in range(4):
        left_part(1 - c, g, snd_sib)
        group = pl.ds(4 * g, 4)
        swaps.append(
            go(remote(snd_sib.at[group], rcv_sib.at[group], a_send.at[g], a_recv.at[g], sibling))
        )
    for g in range(4):
        left_part(c, g, mine)
    for swap in swaps:
        swap.wait_recv()

    near_last = (2, 1, 3)
    near_first = (1, 3, 2)
    after, before = first_peer(1), first_peer(3)

    def group_of(off, half):
        return pl.ds(4 * lax.rem(p1 + off, SIDE) + 2 * half, 2)

    def add_sibling(off):
        group = pl.ds(4 * lax.rem(p1 + off, SIDE), 4)
        mine[group] += rcv_sib[group]

    def ring(group, slot, dev):
        return go(remote(mine.at[group], recv1.at[slot], b_send.at[slot], b_recv.at[slot], dev))

    add_sibling(2)
    hops = [ring(group_of(2, 0), 0, after), ring(group_of(2, 1), 3, before)]
    add_sibling(1)
    hops.append(ring(group_of(1, 1), 1, after))
    add_sibling(3)
    hops.append(ring(group_of(3, 0), 4, before))
    add_sibling(0)
    hops[0].wait_recv()
    mine[group_of(1, 0)] += recv1[0]
    hops.append(ring(group_of(1, 0), 2, after))
    hops[1].wait_recv()
    mine[group_of(3, 1)] += recv1[3]
    hops.append(ring(group_of(3, 1), 5, before))
    for hop in hops[2:]:
        hop.wait_recv()
    s1[pl.ds(0, 2)] = mine[group_of(0, 0)] + recv1[2] + recv1[4]
    s1[pl.ds(2, 2)] = mine[group_of(0, 1)] + recv1[1] + recv1[5]

    seconds = {}
    for off in near_last:
        seconds[off] = go(remote(
            s1.at[lax.rem(p2 + off, SIDE)], recv2.at[off - 1],
            c_send.at[off - 1], c_recv.at[off - 1], second_peer(off),
        ))
    total = s1[p2]
    for off in near_first:
        seconds[off].wait_recv()
        total = total + recv2[off - 1]
    s2[...] = total

    far_first = (4, 3, 5, 2, 6, 1, 7)
    far_last = far_first[::-1]

    def eight(i):
        return pl.ds(pl.multiple_of(8 * i, 8), 8)

    reps = {}
    for off in far_first:
        reps[off] = go(remote(
            s2.at[eight(lax.rem(z + off, REPS)), :], recv3.at[off - 1],
            z_send.at[off - 1], z_recv.at[off - 1], rep_peer(off),
        ))
    total = s2[eight(z), :]
    for off in far_last:
        reps[off].wait_recv()
        total = total + recv3[off - 1]

    whole[eight(z), :] = total * (1.0 / REPS)
    reps = {}
    for off in far_first:
        reps[off] = go(remote(
            whole.at[eight(z), :], whole.at[eight(z), :],
            gz_send.at[off - 1], gz_recv.at[off - 1], rep_peer(off),
        ))
    for off in far_last:
        reps[off].wait_recv()

    own_block = full.at[c, 4 * p1 + p2]
    own_block[...] = whole[...]
    seconds = {}
    for off in near_last:
        seconds[off] = go(remote(
            own_block, own_block, gb_send.at[off - 1], gb_recv.at[off - 1], second_peer(off)
        ))
    for off in near_first:
        seconds[off].wait_recv()

    def pass_on(off):
        group = full.at[c, pl.ds(4 * lax.rem(p1 + SIDE - off, SIDE), 4)]
        return go(remote(group, group, gs_send.at[off], gs_recv.at[off], sibling))

    own_group = full.at[c, pl.ds(4 * p1, 4)]
    firsts = {}
    for off in near_last:
        firsts[off] = go(remote(
            own_group, own_group, gc_send.at[off - 1], gc_recv.at[off - 1], first_peer(off)
        ))
    passed = [pass_on(0)]
    for off in near_first:
        firsts[off].wait_recv()
        passed.append(pass_on(off))

    lane = lax.broadcasted_iota(jnp.int32, (RANK, 128), 1)
    row = lax.broadcasted_iota(jnp.int32, (RANK, 128), 0)

    def split_left(k):
        left = jnp.concatenate([full[k, i] for i in range(16)], axis=1)
        high = left.astype(BF16)
        rows = pl.ds(pl.multiple_of(RANK * k, RANK), RANK)
        lsplit[0, rows, :] = high
        lsplit[1, rows, :] = (left - high.astype(F32)).astype(BF16)

    def left_terms(k):
        rows = pl.ds(pl.multiple_of(RANK * k, RANK), RANK)
        return jnp.concatenate([lsplit[0, rows, :], lsplit[1, rows, :]], axis=0)

    def product(k):
        part = lax.dot_general(dsplit[k], left_terms(k), NT, preferred_element_type=F32)
        part = part[:HID] + part[HID:]
        part = part + pltpu.roll(part, RANK, 1)
        wide = lax.broadcasted_iota(jnp.int32, (HID // 2, 128), 1)
        return jnp.where(wide < RANK, part[: HID // 2], part[HID // 2 :])

    def p_rows(i):
        return pl.ds(pl.multiple_of(16 * i, 16), 16)

    def scatter(slot, k):
        psum[slot, pl.ds(0, HID // 2), :] = product(k)
        psum[slot, pl.ds(HID // 2, 16), :] = jnp.zeros((16, 128), F32)
        out = {}
        for off in far_first:
            n = 7 * slot + off - 1
            out[off] = go(remote(
                psum.at[slot, p_rows(lax.rem(z + off, REPS)), :], recv4.at[slot, off - 1],
                pz_send.at[n], pz_recv.at[n], rep_peer(off),
            ))
        return out

    split_left(c)
    parts = [scatter(0, c)]
    for copy in passed:
        copy.wait_recv()
    split_left(1 - c)
    parts.append(scatter(1, 1 - c))
    store_left.start()

    tables = []
    for k in range(2):
        terms = left_terms(k)
        gram = lax.dot_general(terms, terms, NT, preferred_element_type=F32)
        gram = gram[:RANK] + gram[RANK:]
        gram = gram + pltpu.roll(gram, RANK, 1)
        tables.append(jnp.where(lane < RANK, gram, jnp.where(lane == row + RANK, 1.0, 0.0)))

    def eliminate(j):
        for k in range(2):
            table = tables[k]
            inv = lax.rsqrt(table[j : j + 1, j : j + 1])
            scaled = table[j : j + 1, :] * inv
            factor = jnp.where(row[:, :1] > j, table[:, j : j + 1] * inv, 0.0)
            tables[k] = jnp.where(row == j, scaled, table - factor * scaled)

    for j in range(RANK // 2):
        eliminate(j)

    for slot in range(2):
        total = psum[slot, p_rows(z), :]
        for off in far_last:
            parts[slot][off].wait_recv()
            total = total + recv4[slot, off - 1]
        pfull[slot, p_rows(z), :] = total * (1.0 / REPS)
    reps = {}
    for off in far_first:
        reps[off] = go(remote(
            pfull.at[:, p_rows(z), :], pfull.at[:, p_rows(z), :],
            pg_send.at[off - 1], pg_recv.at[off - 1], rep_peer(off),
        ))

    for j in range(RANK // 2, RANK):
        eliminate(j)

    inverse0 = jnp.where(lane < RANK, pltpu.roll(tables[0], RANK, 1), 0.0)
    inverse1 = jnp.where(lane >= RANK, tables[1], 0.0)
    solve_out[pl.ds(0, RANK), :] = inverse0
    solve_out[pl.ds(RANK, RANK), :] = inverse1
    both = jnp.concatenate([inverse0, inverse1], axis=0)
    solve_out[pl.ds(2 * RANK, 2 * RANK), :] = jnp.dot(
        both.T, both, precision=highest, preferred_element_type=F32
    )

    for off in far_last:
        reps[off].wait_recv()
    own, other = pfull[0, pl.ds(0, HID // 2), :], pfull[1, pl.ds(0, HID // 2), :]
    gate = jnp.where(c == 0, own, other)
    gate = jnp.concatenate([gate, pltpu.roll(gate, RANK, 1)], axis=0)
    raised = jnp.where(c == 0, other, own)
    raised = jnp.concatenate([pltpu.roll(raised, RANK, 1), raised], axis=0)
    wide = lax.broadcasted_iota(jnp.int32, (HID, 128), 1)
    p_out[...] = jnp.where(wide < RANK, gate, raised)

    drain()


AG_SENDS = 30


def step_call(tokens, upstream, weight, feedback, right_factor):
    any_space = pl.BlockSpec(memory_space=pl.ANY)
    vmem = pl.BlockSpec(memory_space=pltpu.VMEM)
    dma = pltpu.SemaphoreType.DMA
    return pl.pallas_call(
        step_kernel,
        name="gather_reduce",
        out_shape=(
            jax.ShapeDtypeStruct((2 * HID, DIM), F32),
            jax.ShapeDtypeStruct((2, 2 * RANK, DIM), BF16),
            jax.ShapeDtypeStruct((256, 128), F32),
            jax.ShapeDtypeStruct((HID, 128), F32),
        ),
        in_specs=[any_space] * 5,
        out_specs=(any_space, any_space, vmem, vmem),
        scratch_shapes=[
            pltpu.VMEM((PAIRS, 4 * CHUNK, DIM), BF16),
            pltpu.VMEM((2 * HID, DIM), F32),
            pltpu.VMEM((2 * HID, DIM), BF16),
            pltpu.VMEM((HID, 32 * CHUNK), BF16),
            pltpu.VMEM((2, RANK, HID), F32),
            pltpu.VMEM((2, 2 * RANK, HID), BF16),
            pltpu.VMEM((2, 2 * HID, DIM), BF16),
            pltpu.VMEM((16, RANK, 128), F32),
            pltpu.VMEM((16, RANK, 128), F32),
            pltpu.VMEM((16, RANK, 128), F32),
            pltpu.VMEM((6, 2, RANK, 128), F32),
            pltpu.VMEM((4, RANK, 128), F32),
            pltpu.VMEM((3, RANK, 128), F32),
            pltpu.VMEM((RANK, 128), F32),
            pltpu.VMEM((7, 8, 128), F32),
            pltpu.VMEM((RANK, 128), F32),
            pltpu.VMEM((2, 16, RANK, 128), F32),
            pltpu.VMEM((2, 2 * RANK, DIM), BF16),
            pltpu.VMEM((2, 128, 128), F32),
            pltpu.VMEM((2, 7, 16, 128), F32),
            pltpu.VMEM((2, 128, 128), F32),
            dma((5,)), dma((2,)),
            dma((AG_SENDS,)), dma((UNITS, 2)), dma((UNITS,)), dma((UNITS,)),
            dma((4,)), dma((4,)), dma((6,)), dma((6,)), dma((3,)), dma((3,)), dma((7,)), dma((7,)),
            dma((7,)), dma((7,)), dma((3,)), dma((3,)), dma((3,)), dma((3,)), dma((4,)), dma((4,)),
            dma((14,)), dma((14,)), dma((7,)), dma((7,)), pltpu.SemaphoreType.REGULAR((2,)),
        ],
        compiler_params=pltpu.CompilerParams(
            collective_id=0, has_side_effects=True, vmem_limit_bytes=60 * 1024 * 1024
        ),
    )(
        tokens.reshape(CHUNK, DIM),
        upstream.reshape(HID, 32 * CHUNK),
        weight.reshape(2 * HID, DIM),
        feedback.reshape(2 * HID, DIM),
        jnp.swapaxes(right_factor, 1, 2),
    )


COLS = 512
SLAB = DIM // REPS


def finish_kernel(
    delta_hbm, left_hbm, solve_hbm, p_hbm, mom_hbm, w_hbm, fb_out, mom_out, w_out, right_out,
    delta, left, solve, p, mom, w, wnext, right, coef, in_sem, out_sem,
):
    z = lax.axis_index("rep")
    slab = pl.ds(pl.multiple_of(SLAB * z, SLAB), SLAB)
    loads = [
        pltpu.make_async_copy(solve_hbm, solve, in_sem.at[0]),
        pltpu.make_async_copy(p_hbm, p, in_sem.at[1]),
    ]
    loads += [
        pltpu.make_async_copy(left_hbm.at[t], left.at[pl.ds(2 * RANK * i, 2 * RANK)], in_sem.at[2 + i])
        for i, t in enumerate((0, 1, 0))
    ]
    chunks = [pl.ds(COLS * j, COLS) for j in range(DIM // COLS)]
    for j, cols in enumerate(chunks):
        loads.append(
            pltpu.make_async_copy(delta_hbm.at[:, :, cols], delta.at[:, :, cols], in_sem.at[5 + j])
        )
    late = 5 + len(chunks)
    loads.append(pltpu.make_async_copy(mom_hbm, mom, in_sem.at[late]))
    loads.append(pltpu.make_async_copy(w_hbm.at[:, :, slab], w, in_sem.at[late + 1]))
    for copy in loads:
        copy.start()
    loads[0].wait()
    loads[1].wait()

    rows = p[...]
    weights = lax.dot_general(
        rows, solve[pl.ds(2 * RANK, 2 * RANK), :], NT,
        precision=highest, preferred_element_type=F32,
    )
    lane = lax.broadcasted_iota(jnp.int32, (HID, 128), 1)
    for k in range(2):
        own = jnp.where((lane < RANK) == (k == 0), weights, 0.0)
        high = own.astype(BF16)
        low = (own - high.astype(F32)).astype(BF16)
        coef[pl.ds(k * HID, HID), :] = jnp.concatenate([high, high, low], axis=1)
    for copy in loads[2:5]:
        copy.wait()

    def approx_at(cols):
        return jnp.dot(coef[...], left[:, cols], preferred_element_type=F32)

    stores = []
    for j, cols in enumerate(chunks):
        approx = approx_at(cols)
        loads[5 + j].wait()
        for k in range(2):
            delta[k, :, cols] = delta[k, :, cols] - approx[k * HID : (k + 1) * HID]
        stores.append(
            pltpu.make_async_copy(delta.at[:, :, cols], fb_out.at[:, :, cols], out_sem.at[j])
        )
        stores[-1].start()

    approx = approx_at(slab)
    loads[late].wait()
    loads[late + 1].wait()
    for k in range(2):
        moved = momentum_decay * mom[k] + approx[k * HID : (k + 1) * HID]
        mom[k] = moved
        wnext[k] = (w[k].astype(F32) - step_rate * moved).astype(BF16)
    turned = lax.dot_general(
        solve[pl.ds(0, 2 * RANK), :], rows, NT, precision=highest, preferred_element_type=F32
    )
    right[0] = turned[:RANK]
    right[1] = turned[RANK:]
    n = len(chunks)
    stores.append(pltpu.make_async_copy(mom, mom_out, out_sem.at[n]))
    stores.append(pltpu.make_async_copy(wnext, w_out, out_sem.at[n + 1]))
    stores.append(pltpu.make_async_copy(right, right_out, out_sem.at[n + 2]))
    for copy in stores[n:]:
        copy.start()
    for copy in stores:
        copy.wait()


def finish_call(delta, left, solve, p, momentum, weight):
    any_space = pl.BlockSpec(memory_space=pl.ANY)
    dma = pltpu.SemaphoreType.DMA
    n = DIM // COLS
    return pl.pallas_call(
        finish_kernel,
        name="finish",
        in_specs=[any_space] * 6,
        out_specs=(any_space,) * 4,
        out_shape=(
            jax.ShapeDtypeStruct((2, HID, DIM), F32),
            jax.ShapeDtypeStruct((2, HID, SLAB), F32),
            jax.ShapeDtypeStruct((2, HID, SLAB), BF16),
            jax.ShapeDtypeStruct((2, RANK, HID), F32),
        ),
        scratch_shapes=[
            pltpu.VMEM((2, HID, DIM), F32),
            pltpu.VMEM((6 * RANK, DIM), BF16),
            pltpu.VMEM((256, 128), F32),
            pltpu.VMEM((HID, 128), F32),
            pltpu.VMEM((2, HID, SLAB), F32),
            pltpu.VMEM((2, HID, SLAB), BF16),
            pltpu.VMEM((2, HID, SLAB), BF16),
            pltpu.VMEM((2, RANK, HID), F32),
            pltpu.VMEM((2 * HID, 6 * RANK), BF16),
            dma((n + 7,)), dma((n + 3,)),
        ],
        compiler_params=pltpu.CompilerParams(vmem_limit_bytes=60 * 1024 * 1024),
    )(delta, left, solve, p, momentum, weight)


def per_device(tokens, upstream, weight, feedback, momentum, right_factor):
    delta, left, solve, p = step_call(tokens, upstream, weight, feedback, right_factor)
    feedback_next, momentum_next, weight_next, right_next = finish_call(
        delta.reshape(2, HID, DIM), left, solve, p, momentum, weight
    )
    return (feedback_next[None], momentum_next, weight_next, jnp.swapaxes(right_next, 1, 2))


def solution(mesh):
    placed = (
        P("rep", "fsdp", None),
        P("rep", "fsdp", None),
        P(None, "fsdp", None),
        P("rep", None, "fsdp", None),
        P(None, "fsdp", "rep"),
        P(None, "fsdp", None),
    )
    return jax.shard_map(
        per_device,
        mesh=mesh,
        in_specs=placed,
        out_specs=(
            P("rep", None, "fsdp", None),
            P(None, "fsdp", "rep"),
            P(None, "fsdp", "rep"),
            P(None, "fsdp", None),
        ),
        check_vma=False,
    )
```

```python
import functools

import jax
import jax.numpy as jnp
from jax import lax
from jax.experimental import pallas as pl
from jax.experimental.pallas import tpu as pltpu
from jax.sharding import PartitionSpec as P

momentum_decay = 0.9
step_rate = 0.05
highest = lax.Precision.HIGHEST
MESH = pl.DeviceIdType.MESH
F32 = jnp.float32
BF16 = jnp.bfloat16

CHUNK = 128
HALF = 64
DIM = 2048
HID = 224
RANK = 64
REPS = 8
SIDE = 4
NT = (((1,), (1,)), ((), ()))

ORDER = [
    (0, 0), (3, 0),
    (1, 0), (0, 3),
    (0, 1), (2, 0),
    (0, 2), (3, 3),
    (1, 1), (1, 3),
    (3, 1), (2, 3),
    (2, 1), (3, 2),
    (1, 2), (2, 2),
]
UNIT = {pos: i for i, pos in enumerate(ORDER)}
UNITS = len(ORDER)
PAIRS = UNITS // 2


def pick(table, u):
    out = jnp.int32(0)
    for i, v in enumerate(table):
        if v:
            out = out + jnp.where(u == i, jnp.int32(v), jnp.int32(0))
    return out


def step_kernel(
    tok_hbm, up_hbm, w_hbm, fb_hbm, rf_hbm,
    delta_out, left_out, solve_out, p_out,
    slots, acc, w, up, rf, r2t, dsplit,
    snd_sib, rcv_sib, mine, recv1, s1, recv2, s2, recv3, whole, full, lsplit, psum, recv4, pfull,
    in_sem, out_sem, ag_send, ag_recv, sib_send, sib_recv,
    a_send, a_recv, b_send, b_recv, c_send, c_recv, z_send, z_recv,
    gz_send, gz_recv, gb_send, gb_recv, gc_send, gc_recv, gs_send, gs_recv,
    pz_send, pz_recv, pg_send, pg_recv, meet_sem,
):
    f = lax.axis_index("fsdp")
    z = lax.axis_index("rep")
    c = lax.rem(f, 2)
    x = lax.rem(lax.div(f, 2), SIDE)
    y = lax.div(f, 2 * SIDE)
    p1 = x * (1 - c) + y * c
    p2 = y * (1 - c) + x * c
    t1 = 2 + 6 * c
    t2 = 8 - 6 * c

    def plane(q1, q2):
        return t1 * lax.rem(p1 + q1, SIDE) + t2 * lax.rem(p2 + q2, SIDE) + c

    def first_peer(off):
        return (plane(off, 0), z)

    def second_peer(off):
        return (plane(0, off), z)

    def rep_peer(off):
        return (f, lax.rem(z + off, REPS))

    sibling = (f + 1 - 2 * c, z)

    def remote(src, dst, ssem, rsem, dev):
        return pltpu.make_async_remote_copy(
            src_ref=src, dst_ref=dst, send_sem=ssem, recv_sem=rsem,
            device_id=dev, device_id_type=MESH,
        )

    load_tok = pltpu.make_async_copy(tok_hbm, slots.at[0, pl.ds(0, CHUNK), :], in_sem.at[0])
    load_tok.start()
    loads = [
        pltpu.make_async_copy(w_hbm, w, in_sem.at[1]),
        pltpu.make_async_copy(up_hbm, up, in_sem.at[2]),
        pltpu.make_async_copy(fb_hbm, acc, in_sem.at[3]),
        pltpu.make_async_copy(rf_hbm, rf, in_sem.at[4]),
    ]
    for copy in loads:
        copy.start()

    barrier = pltpu.get_barrier_semaphore()
    peers = [sibling, first_peer(1), first_peer(3), second_peer(1), second_peer(3)]
    peers += [rep_peer(1), rep_peer(REPS - 1)]

    def meet(turn, off):
        for way in (off, REPS - off):
            pl.semaphore_signal(
                meet_sem.at[turn], inc=1, device_id=rep_peer(way), device_id_type=MESH
            )

    for dev in peers:
        pl.semaphore_signal(barrier, inc=1, device_id=dev, device_id_type=MESH)
    pl.semaphore_wait(barrier, len(peers))
    meet(0, 1)

    started = []

    def piece(d1, d2, h):
        u = UNIT[(d1, d2)]
        return slots.at[u // 2, pl.ds(2 * CHUNK * (u % 2) + HALF * h, HALF), :]

    def send(d1, d2, h, axis, way):
        if axis == 1:
            r1, r2 = (d1 - way) % SIDE, d2
            dev = first_peer(way % SIDE)
        else:
            r1, r2 = d1, (d2 - way) % SIDE
            dev = second_peer(way % SIDE)
        own = d1 == 0 and d2 == 0
        copy = remote(
            tok_hbm.at[pl.ds(HALF * h, HALF), :] if own else piece(d1, d2, h), piece(r1, r2, h),
            ag_send.at[len(started)], ag_recv.at[UNIT[(r1, r2)], h], dev,
        )
        copy.start()
        started.append((d1, d2, h))

    def arrived(d1, d2, h):
        remote(
            piece(d1, d2, h), piece(d1, d2, h),
            ag_send.at[0], ag_recv.at[UNIT[(d1, d2)], h], sibling,
        ).wait_recv()

    def sib_copy(u, half):
        start = 2 * CHUNK * half
        pair = slots.at[lax.div(u, 2)]
        return remote(
            pair.at[pl.ds(start, CHUNK), :], pair.at[pl.ds(start + CHUNK, CHUNK), :],
            sib_send.at[u], sib_recv.at[u], sibling,
        )

    def share(d1, d2):
        u = UNIT[(d1, d2)]
        sib_copy(u, u % 2).start()

    def share_own():
        remote(
            tok_hbm, slots.at[0, pl.ds(CHUNK, CHUNK), :], sib_send.at[0], sib_recv.at[0], sibling
        ).start()

    send(0, 0, 0, 1, 1)
    send(0, 0, 1, 1, -1)
    share_own()
    send(0, 0, 1, 1, 1)
    send(0, 0, 0, 1, -1)
    load_tok.wait()
    for copy in loads:
        copy.wait()

    for k in range(2):
        turned = rf[k]
        high = turned.astype(BF16)
        r2t[k, pl.ds(0, RANK), :] = high
        r2t[k, pl.ds(RANK, RANK), :] = (turned - high.astype(F32)).astype(BF16)

    def actions(step):
        if step == 0:
            arrived(3, 0, 0)
            arrived(1, 0, 1)
            send(3, 0, 0, 1, 1)
            send(1, 0, 1, 1, -1)
            send(0, 0, 0, 2, 1)
            send(0, 0, 1, 2, -1)
            send(0, 0, 1, 2, 1)
            send(0, 0, 0, 2, -1)
            send(3, 0, 0, 2, 1)
            send(1, 0, 1, 2, -1)
            send(1, 0, 1, 2, 1)
            send(3, 0, 0, 2, -1)
            arrived(3, 0, 1)
            arrived(1, 0, 0)
            share(3, 0)
            share(1, 0)
            send(3, 0, 1, 2, 1)
            send(1, 0, 0, 2, -1)
            send(1, 0, 0, 2, 1)
            send(3, 0, 1, 2, -1)
        if step == 1:
            arrived(0, 3, 0)
            arrived(0, 1, 1)
            send(0, 3, 0, 2, 1)
            send(0, 1, 1, 2, -1)
            arrived(0, 3, 1)
            arrived(0, 1, 0)
            share(0, 3)
            share(0, 1)
            arrived(2, 0, 0)
            arrived(2, 0, 1)
            send(2, 0, 0, 2, 1)
            send(2, 0, 1, 2, -1)
            share(2, 0)
        if step == 2:
            arrived(3, 3, 0)
            arrived(1, 1, 1)
            send(3, 3, 0, 2, 1)
            send(1, 1, 1, 2, -1)
            send(2, 0, 1, 2, 1)
            send(2, 0, 0, 2, -1)
            pl.semaphore_wait(meet_sem.at[0], 2)
            meet(1, 2)
        if step == 3:
            arrived(0, 2, 0)
            arrived(0, 2, 1)
            share(0, 2)
            arrived(3, 3, 1)
            arrived(1, 1, 0)
            share(3, 3)
            share(1, 1)
        if step == 4:
            arrived(1, 3, 0)
            arrived(3, 1, 1)
            send(1, 3, 0, 2, 1)
            send(3, 1, 1, 2, -1)
            arrived(1, 3, 1)
            arrived(3, 1, 0)
            share(1, 3)
            share(3, 1)
        if step == 5:
            arrived(2, 3, 0)
            arrived(2, 1, 1)
            send(2, 3, 0, 2, 1)
            send(2, 1, 1, 2, -1)
            arrived(2, 3, 1)
            arrived(2, 1, 0)
            share(2, 3)
            share(2, 1)
            pl.semaphore_wait(meet_sem.at[1], 2)
        if step == 6:
            arrived(3, 2, 0)
            arrived(1, 2, 1)
            arrived(3, 2, 1)
            arrived(1, 2, 0)
            share(3, 2)
            share(1, 2)
        if step == 7:
            arrived(2, 2, 0)
            arrived(2, 2, 1)
            share(2, 2)

    first_of = [d1 for d1, _ in ORDER]
    second_of = [d2 for _, d2 in ORDER]

    def cotangents(u):
        d1, d2 = pick(first_of, u), pick(second_of, u)
        other = t2 * lax.rem(p2 + d1, SIDE) + t1 * lax.rem(p1 + d2, SIDE) + (1 - c)
        return [
            up[:, pl.ds(pl.multiple_of(dev * CHUNK, CHUNK), CHUNK)]
            for dev in (plane(d1, d2), other)
        ]

    def pair_step(step, carry):
        for i in range(PAIRS):
            @pl.when(step == i)
            def _(i=i):
                actions(i)

        for half in range(2):
            sib_copy(2 * step + half, half).wait_recv()
        cot = jnp.concatenate(cotangents(2 * step) + cotangents(2 * step + 1), axis=1).astype(F32)
        rows = slots[step]
        pre = lax.dot_general(w[...], rows, NT, preferred_element_type=F32)
        gate_pre, up_pre = pre[:HID], pre[HID:]
        sig = jax.nn.sigmoid(gate_pre)
        grad_gate = (cot * up_pre * (sig * (1.0 + gate_pre * (1.0 - sig)))).astype(BF16)
        grad_up = (cot * (gate_pre * sig)).astype(BF16)
        grads = jnp.concatenate([grad_gate, grad_up], axis=0)
        acc[...] += jnp.dot(grads, rows, preferred_element_type=F32)
        return carry

    lax.fori_loop(0, PAIRS, pair_step, 0)
    pending = []

    def go(copy):
        copy.start()
        pending.append(copy)
        return copy

    def drain():
        for i, (d1, d2, h) in enumerate(started):
            remote(
                piece(d1, d2, h), piece(d1, d2, h), ag_send.at[i], ag_recv.at[0, 0], sibling
            ).wait_send()
        for u in range(UNITS):
            sib_copy(u, u % 2).wait_send()
        for copy in pending:
            copy.wait_send()
        store_delta.wait()
        store_left.wait()

    store_left = pltpu.make_async_copy(lsplit, left_out, out_sem.at[1])
    store_delta = pltpu.make_async_copy(acc, delta_out, out_sem.at[0])
    store_delta.start()

    def left_part(k, g, dst):
        cols = pl.ds(pl.multiple_of(512 * g, 512), 512)
        block = acc[pl.ds(pl.multiple_of(HID * k, 32), HID), cols]
        high = block.astype(BF16)
        low = (block - high.astype(F32)).astype(BF16)
        dsplit[k, pl.ds(0, HID), cols] = high
        dsplit[k, pl.ds(HID, HID), cols] = low
        both = jnp.dot(r2t[k], high, preferred_element_type=F32)
        part = both[:RANK] + both[RANK:]
        part = part + jnp.dot(r2t[k, pl.ds(0, RANK), :], low, preferred_element_type=F32)
        for i in range(4):
            dst[4 * g + i] = part[:, 128 * i : 128 * (i + 1)]

    near_last = (2, 1, 3)
    near_first = (1, 3, 2)
    swaps = {}
    for n, off in enumerate(near_last + (0,)):
        g = lax.rem(p2 + off, SIDE)
        left_part(1 - c, g, snd_sib)
        group = pl.ds(4 * g, 4)
        swaps[off] = go(
            remote(snd_sib.at[group], rcv_sib.at[group], a_send.at[n], a_recv.at[n], sibling)
        )

    after, before = first_peer(1), first_peer(3)

    def group_of(off, half):
        return pl.ds(4 * lax.rem(p1 + off, SIDE) + 2 * half, 2)

    def add_sibling(off):
        q = lax.rem(p1 + off, SIDE)
        left_part(c, q, mine)
        swaps[off].wait_recv()
        group = pl.ds(4 * q, 4)
        mine[group] += rcv_sib[group]

    def ring(group, slot, dev):
        return go(remote(mine.at[group], recv1.at[slot], b_send.at[slot], b_recv.at[slot], dev))

    add_sibling(2)
    hops = [ring(group_of(2, 0), 0, after), ring(group_of(2, 1), 3, before)]
    add_sibling(1)
    hops.append(ring(group_of(1, 1), 1, after))
    add_sibling(3)
    hops.append(ring(group_of(3, 0), 4, before))
    add_sibling(0)
    hops[0].wait_recv()
    mine[group_of(1, 0)] += recv1[0]
    hops.append(ring(group_of(1, 0), 2, after))
    hops[1].wait_recv()
    mine[group_of(3, 1)] += recv1[3]
    hops.append(ring(group_of(3, 1), 5, before))
    for hop in hops[2:]:
        hop.wait_recv()
    s1[pl.ds(0, 2)] = mine[group_of(0, 0)] + recv1[2] + recv1[4]
    s1[pl.ds(2, 2)] = mine[group_of(0, 1)] + recv1[1] + recv1[5]

    seconds = {}
    for off in near_last:
        seconds[off] = go(remote(
            s1.at[lax.rem(p2 + off, SIDE)], recv2.at[off - 1],
            c_send.at[off - 1], c_recv.at[off - 1], second_peer(off),
        ))
    total = s1[p2]
    for off in near_first:
        seconds[off].wait_recv()
        total = total + recv2[off - 1]
    s2[...] = total

    far_first = (4, 3, 5, 2, 6, 1, 7)
    far_last = far_first[::-1]

    def eight(i):
        return pl.ds(pl.multiple_of(8 * i, 8), 8)

    reps = {}
    for off in far_first:
        reps[off] = go(remote(
            s2.at[eight(lax.rem(z + off, REPS)), :], recv3.at[off - 1],
            z_send.at[off - 1], z_recv.at[off - 1], rep_peer(off),
        ))
    total = s2[eight(z), :]
    for off in far_last:
        reps[off].wait_recv()
        total = total + recv3[off - 1]

    whole[eight(z), :] = total * (1.0 / REPS)
    reps = {}
    for off in far_first:
        reps[off] = go(remote(
            whole.at[eight(z), :], whole.at[eight(z), :],
            gz_send.at[off - 1], gz_recv.at[off - 1], rep_peer(off),
        ))
    for off in far_last:
        reps[off].wait_recv()

    own_block = full.at[c, 4 * p1 + p2]
    own_block[...] = whole[...]
    seconds = {}
    for off in near_last:
        seconds[off] = go(remote(
            own_block, own_block, gb_send.at[off - 1], gb_recv.at[off - 1], second_peer(off)
        ))
    for off in near_first:
        seconds[off].wait_recv()

    def pass_on(off):
        group = full.at[c, pl.ds(4 * lax.rem(p1 + SIDE - off, SIDE), 4)]
        return go(remote(group, group, gs_send.at[off], gs_recv.at[off], sibling))

    lane = lax.broadcasted_iota(jnp.int32, (RANK, 128), 1)
    row = lax.broadcasted_iota(jnp.int32, (RANK, 128), 0)

    def absorb(k, q):
        left = jnp.concatenate([full[k, 4 * q + i] for i in range(4)], axis=1)
        high = left.astype(BF16)
        low = (left - high.astype(F32)).astype(BF16)
        rows = pl.ds(pl.multiple_of(RANK * k, RANK), RANK)
        cols = pl.ds(pl.multiple_of(512 * q, 512), 512)
        lsplit[0, rows, cols] = high
        lsplit[1, rows, cols] = low
        terms = jnp.concatenate([high, low], axis=0)
        part = lax.dot_general(dsplit[k, :, cols], terms, NT, preferred_element_type=F32)
        return part[:HID] + part[HID:]

    def absorb_own(off):
        return absorb(c, lax.rem(p1 + SIDE - off, SIDE))

    def absorb_other(off):
        passed[off].wait_recv()
        return absorb(1 - c, lax.rem(p2 + SIDE - off, SIDE))

    own_group = full.at[c, pl.ds(4 * p1, 4)]
    firsts = {}
    for off in near_last:
        firsts[off] = go(remote(
            own_group, own_group, gc_send.at[off - 1], gc_recv.at[off - 1], first_peer(off)
        ))
    passed = {0: pass_on(0)}
    prod_own = absorb_own(0)
    prod_other = absorb_other(0)
    for off in near_first:
        firsts[off].wait_recv()
        passed[off] = pass_on(off)
        prod_own = prod_own + absorb_own(off)

    def left_terms(k):
        rows = pl.ds(RANK * k, RANK)
        return jnp.concatenate([lsplit[0, rows, :], lsplit[1, rows, :]], axis=0)

    def packed(part):
        part = part + pltpu.roll(part, RANK, 1)
        wide = lax.broadcasted_iota(jnp.int32, (HID // 2, 128), 1)
        return jnp.where(wide < RANK, part[: HID // 2], part[HID // 2 :])

    def p_rows(i):
        return pl.ds(pl.multiple_of(16 * i, 16), 16)

    def scatter(slot, part):
        psum[slot, pl.ds(0, HID // 2), :] = packed(part)
        psum[slot, pl.ds(HID // 2, 16), :] = jnp.zeros((16, 128), F32)
        out = {}
        for off in far_first:
            n = 7 * slot + off - 1
            out[off] = go(remote(
                psum.at[slot, p_rows(lax.rem(z + off, REPS)), :], recv4.at[slot, off - 1],
                pz_send.at[n], pz_recv.at[n], rep_peer(off),
            ))
        return out

    parts = [scatter(0, prod_own)]
    for off in near_first:
        prod_other = prod_other + absorb_other(off)
    parts.append(scatter(1, prod_other))
    store_left.start()

    tables = []
    for k in range(2):
        terms = left_terms(k)
        gram = lax.dot_general(terms, terms, NT, preferred_element_type=F32)
        gram = gram[:RANK] + gram[RANK:]
        gram = gram + pltpu.roll(gram, RANK, 1)
        tables.append(jnp.where(lane < RANK, gram, jnp.where(lane == row + RANK, 1.0, 0.0)))

    def eliminate(j):
        for k in range(2):
            table = tables[k]
            inv = lax.rsqrt(table[j : j + 1, j : j + 1])
            scaled = table[j : j + 1, :] * inv
            factor = jnp.where(row[:, :1] > j, table[:, j : j + 1] * inv, 0.0)
            tables[k] = jnp.where(row == j, scaled, table - factor * scaled)

    for j in range(RANK // 2):
        eliminate(j)

    for slot in range(2):
        total = psum[slot, p_rows(z), :]
        for off in far_last:
            parts[slot][off].wait_recv()
            total = total + recv4[slot, off - 1]
        pfull[slot, p_rows(z), :] = total * (1.0 / REPS)
    reps = {}
    for off in far_first:
        reps[off] = go(remote(
            pfull.at[:, p_rows(z), :], pfull.at[:, p_rows(z), :],
            pg_send.at[off - 1], pg_recv.at[off - 1], rep_peer(off),
        ))

    for j in range(RANK // 2, RANK):
        eliminate(j)

    inverse0 = jnp.where(lane < RANK, pltpu.roll(tables[0], RANK, 1), 0.0)
    inverse1 = jnp.where(lane >= RANK, tables[1], 0.0)
    solve_out[pl.ds(0, RANK), :] = inverse0
    solve_out[pl.ds(RANK, RANK), :] = inverse1
    both = jnp.concatenate([inverse0, inverse1], axis=0)
    solve_out[pl.ds(2 * RANK, 2 * RANK), :] = jnp.dot(
        both.T, both, precision=highest, preferred_element_type=F32
    )

    for off in far_last:
        reps[off].wait_recv()
    own, other = pfull[0, pl.ds(0, HID // 2), :], pfull[1, pl.ds(0, HID // 2), :]
    gate = jnp.where(c == 0, own, other)
    gate = jnp.concatenate([gate, pltpu.roll(gate, RANK, 1)], axis=0)
    raised = jnp.where(c == 0, other, own)
    raised = jnp.concatenate([pltpu.roll(raised, RANK, 1), raised], axis=0)
    wide = lax.broadcasted_iota(jnp.int32, (HID, 128), 1)
    p_out[...] = jnp.where(wide < RANK, gate, raised)

    drain()


AG_SENDS = 30


def step_call(tokens, upstream, weight, feedback, right_factor):
    any_space = pl.BlockSpec(memory_space=pl.ANY)
    vmem = pl.BlockSpec(memory_space=pltpu.VMEM)
    dma = pltpu.SemaphoreType.DMA
    return pl.pallas_call(
        step_kernel,
        name="gather_reduce",
        out_shape=(
            jax.ShapeDtypeStruct((2 * HID, DIM), F32),
            jax.ShapeDtypeStruct((2, 2 * RANK, DIM), BF16),
            jax.ShapeDtypeStruct((256, 128), F32),
            jax.ShapeDtypeStruct((HID, 128), F32),
        ),
        in_specs=[any_space] * 5,
        out_specs=(any_space, any_space, vmem, vmem),
        scratch_shapes=[
            pltpu.VMEM((PAIRS, 4 * CHUNK, DIM), BF16),
            pltpu.VMEM((2 * HID, DIM), F32),
            pltpu.VMEM((2 * HID, DIM), BF16),
            pltpu.VMEM((HID, 32 * CHUNK), BF16),
            pltpu.VMEM((2, RANK, HID), F32),
            pltpu.VMEM((2, 2 * RANK, HID), BF16),
            pltpu.VMEM((2, 2 * HID, DIM), BF16),
            pltpu.VMEM((16, RANK, 128), F32),
            pltpu.VMEM((16, RANK, 128), F32),
            pltpu.VMEM((16, RANK, 128), F32),
            pltpu.VMEM((6, 2, RANK, 128), F32),
            pltpu.VMEM((4, RANK, 128), F32),
            pltpu.VMEM((3, RANK, 128), F32),
            pltpu.VMEM((RANK, 128), F32),
            pltpu.VMEM((7, 8, 128), F32),
            pltpu.VMEM((RANK, 128), F32),
            pltpu.VMEM((2, 16, RANK, 128), F32),
            pltpu.VMEM((2, 2 * RANK, DIM), BF16),
            pltpu.VMEM((2, 128, 128), F32),
            pltpu.VMEM((2, 7, 16, 128), F32),
            pltpu.VMEM((2, 128, 128), F32),
            dma((5,)), dma((2,)),
            dma((AG_SENDS,)), dma((UNITS, 2)), dma((UNITS,)), dma((UNITS,)),
            dma((4,)), dma((4,)), dma((6,)), dma((6,)), dma((3,)), dma((3,)), dma((7,)), dma((7,)),
            dma((7,)), dma((7,)), dma((3,)), dma((3,)), dma((3,)), dma((3,)), dma((4,)), dma((4,)),
            dma((14,)), dma((14,)), dma((7,)), dma((7,)), pltpu.SemaphoreType.REGULAR((2,)),
        ],
        compiler_params=pltpu.CompilerParams(
            collective_id=0, has_side_effects=True, vmem_limit_bytes=60 * 1024 * 1024
        ),
    )(
        tokens.reshape(CHUNK, DIM),
        upstream.reshape(HID, 32 * CHUNK),
        weight.reshape(2 * HID, DIM),
        feedback.reshape(2 * HID, DIM),
        jnp.swapaxes(right_factor, 1, 2),
    )


COLS = 512
SLAB = DIM // REPS


def finish_kernel(
    delta_hbm, left_hbm, solve_hbm, p_hbm, mom_hbm, w_hbm, fb_out, mom_out, w_out, right_out,
    delta, left, solve, p, mom, w, wnext, right, coef, in_sem, out_sem,
):
    z = lax.axis_index("rep")
    slab = pl.ds(pl.multiple_of(SLAB * z, SLAB), SLAB)
    loads = [
        pltpu.make_async_copy(solve_hbm, solve, in_sem.at[0]),
        pltpu.make_async_copy(p_hbm, p, in_sem.at[1]),
    ]
    loads += [
        pltpu.make_async_copy(left_hbm.at[t], left.at[pl.ds(2 * RANK * i, 2 * RANK)], in_sem.at[2 + i])
        for i, t in enumerate((0, 1, 0))
    ]
    chunks = [pl.ds(COLS * j, COLS) for j in range(DIM // COLS)]
    for j, cols in enumerate(chunks):
        loads.append(
            pltpu.make_async_copy(delta_hbm.at[:, :, cols], delta.at[:, :, cols], in_sem.at[5 + j])
        )
    late = 5 + len(chunks)
    loads.append(pltpu.make_async_copy(mom_hbm, mom, in_sem.at[late]))
    loads.append(pltpu.make_async_copy(w_hbm.at[:, :, slab], w, in_sem.at[late + 1]))
    for copy in loads:
        copy.start()
    loads[0].wait()
    loads[1].wait()

    rows = p[...]
    weights = lax.dot_general(
        rows, solve[pl.ds(2 * RANK, 2 * RANK), :], NT,
        precision=highest, preferred_element_type=F32,
    )
    lane = lax.broadcasted_iota(jnp.int32, (HID, 128), 1)
    for k in range(2):
        own = jnp.where((lane < RANK) == (k == 0), weights, 0.0)
        high = own.astype(BF16)
        low = (own - high.astype(F32)).astype(BF16)
        coef[pl.ds(k * HID, HID), :] = jnp.concatenate([high, high, low], axis=1)
    for copy in loads[2:5]:
        copy.wait()

    def approx_at(cols):
        return jnp.dot(coef[...], left[:, cols], preferred_element_type=F32)

    stores = []

    def store(src, dst):
        stores.append(pltpu.make_async_copy(src, dst, out_sem.at[len(stores)]))
        stores[-1].start()

    for j, cols in enumerate(chunks):
        approx = approx_at(cols)
        loads[5 + j].wait()
        for k in range(2):
            delta[k, :, cols] = delta[k, :, cols] - approx[k * HID : (k + 1) * HID]
        store(delta.at[:, :, cols], fb_out.at[:, :, cols])
        if j == 0:
            turned = lax.dot_general(
                solve[pl.ds(0, 2 * RANK), :], rows, NT,
                precision=highest, preferred_element_type=F32,
            )
            right[0] = turned[:RANK]
            right[1] = turned[RANK:]
            store(right, right_out)
            approx = approx_at(slab)
            loads[late].wait()
            loads[late + 1].wait()
            for k in range(2):
                moved = momentum_decay * mom[k] + approx[k * HID : (k + 1) * HID]
                mom[k] = moved
                wnext[k] = (w[k].astype(F32) - step_rate * moved).astype(BF16)
            store(mom, mom_out)
            store(wnext, w_out)
    for copy in stores:
        copy.wait()


def finish_call(delta, left, solve, p, momentum, weight):
    any_space = pl.BlockSpec(memory_space=pl.ANY)
    dma = pltpu.SemaphoreType.DMA
    n = DIM // COLS
    return pl.pallas_call(
        finish_kernel,
        name="finish",
        in_specs=[any_space] * 6,
        out_specs=(any_space,) * 4,
        out_shape=(
            jax.ShapeDtypeStruct((2, HID, DIM), F32),
            jax.ShapeDtypeStruct((2, HID, SLAB), F32),
            jax.ShapeDtypeStruct((2, HID, SLAB), BF16),
            jax.ShapeDtypeStruct((2, RANK, HID), F32),
        ),
        scratch_shapes=[
            pltpu.VMEM((2, HID, DIM), F32),
            pltpu.VMEM((6 * RANK, DIM), BF16),
            pltpu.VMEM((256, 128), F32),
            pltpu.VMEM((HID, 128), F32),
            pltpu.VMEM((2, HID, SLAB), F32),
            pltpu.VMEM((2, HID, SLAB), BF16),
            pltpu.VMEM((2, HID, SLAB), BF16),
            pltpu.VMEM((2, RANK, HID), F32),
            pltpu.VMEM((2 * HID, 6 * RANK), BF16),
            dma((n + 7,)), dma((n + 3,)),
        ],
        compiler_params=pltpu.CompilerParams(vmem_limit_bytes=60 * 1024 * 1024),
    )(delta, left, solve, p, momentum, weight)


def per_device(tokens, upstream, weight, feedback, momentum, right_factor):
    delta, left, solve, p = step_call(tokens, upstream, weight, feedback, right_factor)
    feedback_next, momentum_next, weight_next, right_next = finish_call(
        delta.reshape(2, HID, DIM), left, solve, p, momentum, weight
    )
    return (feedback_next[None], momentum_next, weight_next, jnp.swapaxes(right_next, 1, 2))


def solution(mesh):
    placed = (
        P("rep", "fsdp", None),
        P("rep", "fsdp", None),
        P(None, "fsdp", None),
        P("rep", None, "fsdp", None),
        P(None, "fsdp", "rep"),
        P(None, "fsdp", None),
    )
    return jax.shard_map(
        per_device,
        mesh=mesh,
        in_specs=placed,
        out_specs=(
            P("rep", None, "fsdp", None),
            P(None, "fsdp", "rep"),
            P(None, "fsdp", "rep"),
            P(None, "fsdp", None),
        ),
        check_vma=False,
    )
```

```python
import functools

import jax
import jax.numpy as jnp
from jax import lax
from jax.experimental import pallas as pl
from jax.experimental.pallas import tpu as pltpu
from jax.sharding import PartitionSpec as P

momentum_decay = 0.9
step_rate = 0.05
highest = lax.Precision.HIGHEST
MESH = pl.DeviceIdType.MESH
F32 = jnp.float32
BF16 = jnp.bfloat16

CHUNK = 128
HALF = 64
DIM = 2048
HID = 224
RANK = 64
REPS = 8
SIDE = 4
NT = (((1,), (1,)), ((), ()))

ORDER = [
    (0, 0), (3, 0),
    (1, 0), (0, 3),
    (0, 1), (2, 0),
    (0, 2), (3, 3),
    (1, 1), (1, 3),
    (3, 1), (2, 3),
    (2, 1), (3, 2),
    (1, 2), (2, 2),
]
UNIT = {pos: i for i, pos in enumerate(ORDER)}
UNITS = len(ORDER)
PAIRS = UNITS // 2


def pick(table, u):
    out = jnp.int32(0)
    for i, v in enumerate(table):
        if v:
            out = out + jnp.where(u == i, jnp.int32(v), jnp.int32(0))
    return out


def step_kernel(
    tok_hbm, up_hbm, w_hbm, fb_hbm, rf_hbm,
    delta_out, left_out, solve_out, p_out,
    slots, acc, w, up, rf, r2t, dsplit,
    snd_sib, rcv_sib, mine, recv1, s1, recv2, s2, recv3, whole, full, lsplit, psum, recv4, pfull,
    in_sem, out_sem, ag_send, ag_recv, sib_send, sib_recv,
    a_send, a_recv, b_send, b_recv, c_send, c_recv, z_send, z_recv,
    gz_send, gz_recv, gb_send, gb_recv, gc_send, gc_recv, gs_send, gs_recv,
    pz_send, pz_recv, pg_send, pg_recv, meet_sem,
):
    f = lax.axis_index("fsdp")
    z = lax.axis_index("rep")
    c = lax.rem(f, 2)
    x = lax.rem(lax.div(f, 2), SIDE)
    y = lax.div(f, 2 * SIDE)
    p1 = x * (1 - c) + y * c
    p2 = y * (1 - c) + x * c
    t1 = 2 + 6 * c
    t2 = 8 - 6 * c

    def plane(q1, q2):
        return t1 * lax.rem(p1 + q1, SIDE) + t2 * lax.rem(p2 + q2, SIDE) + c

    def first_peer(off):
        return (plane(off, 0), z)

    def second_peer(off):
        return (plane(0, off), z)

    def rep_peer(off):
        return (f, lax.rem(z + off, REPS))

    sibling = (f + 1 - 2 * c, z)

    def remote(src, dst, ssem, rsem, dev):
        return pltpu.make_async_remote_copy(
            src_ref=src, dst_ref=dst, send_sem=ssem, recv_sem=rsem,
            device_id=dev, device_id_type=MESH,
        )

    load_tok = pltpu.make_async_copy(tok_hbm, slots.at[0, pl.ds(0, CHUNK), :], in_sem.at[0])
    load_tok.start()
    loads = [
        pltpu.make_async_copy(w_hbm, w, in_sem.at[1]),
        pltpu.make_async_copy(up_hbm, up, in_sem.at[2]),
        pltpu.make_async_copy(fb_hbm, acc, in_sem.at[3]),
        pltpu.make_async_copy(rf_hbm, rf, in_sem.at[4]),
    ]
    for copy in loads:
        copy.start()

    barrier = pltpu.get_barrier_semaphore()
    peers = [sibling, first_peer(1), first_peer(3), second_peer(1), second_peer(3)]
    peers += [rep_peer(1), rep_peer(REPS - 1)]

    def meet(turn, off):
        for way in (off, REPS - off):
            pl.semaphore_signal(
                meet_sem.at[turn], inc=1, device_id=rep_peer(way), device_id_type=MESH
            )

    for dev in peers:
        pl.semaphore_signal(barrier, inc=1, device_id=dev, device_id_type=MESH)
    pl.semaphore_wait(barrier, len(peers))
    meet(0, 1)

    started = []

    def piece(d1, d2, h):
        u = UNIT[(d1, d2)]
        return slots.at[u // 2, pl.ds(2 * CHUNK * (u % 2) + HALF * h, HALF), :]

    def send(d1, d2, h, axis, way):
        if axis == 1:
            r1, r2 = (d1 - way) % SIDE, d2
            dev = first_peer(way % SIDE)
        else:
            r1, r2 = d1, (d2 - way) % SIDE
            dev = second_peer(way % SIDE)
        own = d1 == 0 and d2 == 0
        copy = remote(
            tok_hbm.at[pl.ds(HALF * h, HALF), :] if own else piece(d1, d2, h), piece(r1, r2, h),
            ag_send.at[len(started)], ag_recv.at[UNIT[(r1, r2)], h], dev,
        )
        copy.start()
        started.append((d1, d2, h))

    def arrived(d1, d2, h):
        remote(
            piece(d1, d2, h), piece(d1, d2, h),
            ag_send.at[0], ag_recv.at[UNIT[(d1, d2)], h], sibling,
        ).wait_recv()

    def sib_copy(u, half):
        start = 2 * CHUNK * half
        pair = slots.at[lax.div(u, 2)]
        return remote(
            pair.at[pl.ds(start, CHUNK), :], pair.at[pl.ds(start + CHUNK, CHUNK), :],
            sib_send.at[u], sib_recv.at[u], sibling,
        )

    def share(d1, d2):
        u = UNIT[(d1, d2)]
        sib_copy(u, u % 2).start()

    def share_own():
        remote(
            tok_hbm, slots.at[0, pl.ds(CHUNK, CHUNK), :], sib_send.at[0], sib_recv.at[0], sibling
        ).start()

    send(0, 0, 0, 1, 1)
    send(0, 0, 1, 1, -1)
    share_own()
    send(0, 0, 1, 1, 1)
    send(0, 0, 0, 1, -1)
    load_tok.wait()
    for copy in loads:
        copy.wait()

    for k in range(2):
        turned = rf[k]
        high = turned.astype(BF16)
        r2t[k, pl.ds(0, RANK), :] = high
        r2t[k, pl.ds(RANK, RANK), :] = (turned - high.astype(F32)).astype(BF16)

    def actions(step):
        if step == 0:
            arrived(3, 0, 0)
            arrived(1, 0, 1)
            send(3, 0, 0, 1, 1)
            send(1, 0, 1, 1, -1)
            send(0, 0, 0, 2, 1)
            send(0, 0, 1, 2, -1)
            send(0, 0, 1, 2, 1)
            send(0, 0, 0, 2, -1)
            send(3, 0, 0, 2, 1)
            send(1, 0, 1, 2, -1)
            send(1, 0, 1, 2, 1)
            send(3, 0, 0, 2, -1)
            arrived(3, 0, 1)
            arrived(1, 0, 0)
            share(3, 0)
            share(1, 0)
            send(3, 0, 1, 2, 1)
            send(1, 0, 0, 2, -1)
            send(1, 0, 0, 2, 1)
            send(3, 0, 1, 2, -1)
        if step == 1:
            arrived(0, 3, 0)
            arrived(0, 1, 1)
            send(0, 3, 0, 2, 1)
            send(0, 1, 1, 2, -1)
            arrived(0, 3, 1)
            arrived(0, 1, 0)
            share(0, 3)
            share(0, 1)
            arrived(2, 0, 0)
            arrived(2, 0, 1)
            send(2, 0, 0, 2, 1)
            send(2, 0, 1, 2, -1)
            share(2, 0)
        if step == 2:
            arrived(3, 3, 0)
            arrived(1, 1, 1)
            send(3, 3, 0, 2, 1)
            send(1, 1, 1, 2, -1)
            send(2, 0, 1, 2, 1)
            send(2, 0, 0, 2, -1)
            pl.semaphore_wait(meet_sem.at[0], 2)
            meet(1, 2)
        if step == 3:
            arrived(0, 2, 0)
            arrived(0, 2, 1)
            share(0, 2)
            arrived(3, 3, 1)
            arrived(1, 1, 0)
            share(3, 3)
            share(1, 1)
        if step == 4:
            arrived(1, 3, 0)
            arrived(3, 1, 1)
            send(1, 3, 0, 2, 1)
            send(3, 1, 1, 2, -1)
            arrived(1, 3, 1)
            arrived(3, 1, 0)
            share(1, 3)
            share(3, 1)
        if step == 5:
            arrived(2, 3, 0)
            arrived(2, 1, 1)
            send(2, 3, 0, 2, 1)
            send(2, 1, 1, 2, -1)
            arrived(2, 3, 1)
            arrived(2, 1, 0)
            share(2, 3)
            share(2, 1)
            pl.semaphore_wait(meet_sem.at[1], 2)
        if step == 6:
            arrived(3, 2, 0)
            arrived(1, 2, 1)
            arrived(3, 2, 1)
            arrived(1, 2, 0)
            share(3, 2)
            share(1, 2)
        if step == 7:
            arrived(2, 2, 0)
            arrived(2, 2, 1)
            share(2, 2)

    first_of = [d1 for d1, _ in ORDER]
    second_of = [d2 for _, d2 in ORDER]

    def cotangents(u):
        d1, d2 = pick(first_of, u), pick(second_of, u)
        other = t2 * lax.rem(p2 + d1, SIDE) + t1 * lax.rem(p1 + d2, SIDE) + (1 - c)
        return [
            up[:, pl.ds(pl.multiple_of(dev * CHUNK, CHUNK), CHUNK)]
            for dev in (plane(d1, d2), other)
        ]

    def pair_step(step, carry):
        for i in range(PAIRS):
            @pl.when(step == i)
            def _(i=i):
                actions(i)

        for half in range(2):
            sib_copy(2 * step + half, half).wait_recv()
        cot = jnp.concatenate(cotangents(2 * step) + cotangents(2 * step + 1), axis=1).astype(F32)
        rows = slots[step]
        pre = lax.dot_general(w[...], rows, NT, preferred_element_type=F32)
        gate_pre, up_pre = pre[:HID], pre[HID:]
        sig = jax.nn.sigmoid(gate_pre)
        grad_gate = (cot * up_pre * (sig * (1.0 + gate_pre * (1.0 - sig)))).astype(BF16)
        grad_up = (cot * (gate_pre * sig)).astype(BF16)
        grads = jnp.concatenate([grad_gate, grad_up], axis=0)
        acc[...] += jnp.dot(grads, rows, preferred_element_type=F32)
        return carry

    lax.fori_loop(0, PAIRS, pair_step, 0)
    pending = []

    def go(copy):
        copy.start()
        pending.append(copy)
        return copy

    def drain():
        for i, (d1, d2, h) in enumerate(started):
            remote(
                piece(d1, d2, h), piece(d1, d2, h), ag_send.at[i], ag_recv.at[0, 0], sibling
            ).wait_send()
        for u in range(UNITS):
            sib_copy(u, u % 2).wait_send()
        for copy in pending:
            copy.wait_send()
        store_delta.wait()
        store_left.wait()

    store_left = pltpu.make_async_copy(lsplit, left_out, out_sem.at[1])
    store_delta = pltpu.make_async_copy(acc, delta_out, out_sem.at[0])
    store_delta.start()

    def left_part(k, g, dst):
        cols = pl.ds(pl.multiple_of(512 * g, 512), 512)
        block = acc[pl.ds(pl.multiple_of(HID * k, 32), HID), cols]
        high = block.astype(BF16)
        low = (block - high.astype(F32)).astype(BF16)
        dsplit[k, pl.ds(0, HID), cols] = high
        dsplit[k, pl.ds(HID, HID), cols] = low
        both = jnp.dot(r2t[k], high, preferred_element_type=F32)
        part = both[:RANK] + both[RANK:]
        part = part + jnp.dot(r2t[k, pl.ds(0, RANK), :], low, preferred_element_type=F32)
        for i in range(4):
            dst[4 * g + i] = part[:, 128 * i : 128 * (i + 1)]

    near_last = (2, 1, 3)
    near_first = (1, 3, 2)
    swaps = {}
    for n, off in enumerate(near_last + (0,)):
        g = lax.rem(p2 + off, SIDE)
        left_part(1 - c, g, snd_sib)
        group = pl.ds(4 * g, 4)
        swaps[off] = go(
            remote(snd_sib.at[group], rcv_sib.at[group], a_send.at[n], a_recv.at[n], sibling)
        )

    after, before = first_peer(1), first_peer(3)

    def group_of(off, half):
        return pl.ds(4 * lax.rem(p1 + off, SIDE) + 2 * half, 2)

    def add_sibling(off):
        q = lax.rem(p1 + off, SIDE)
        left_part(c, q, mine)
        swaps[off].wait_recv()
        group = pl.ds(4 * q, 4)
        mine[group] += rcv_sib[group]

    def ring(group, slot, dev):
        return go(remote(mine.at[group], recv1.at[slot], b_send.at[slot], b_recv.at[slot], dev))

    add_sibling(2)
    hops = [ring(group_of(2, 0), 0, after), ring(group_of(2, 1), 3, before)]
    add_sibling(1)
    hops.append(ring(group_of(1, 1), 1, after))
    add_sibling(3)
    hops.append(ring(group_of(3, 0), 4, before))
    add_sibling(0)
    hops[0].wait_recv()
    mine[group_of(1, 0)] += recv1[0]
    hops.append(ring(group_of(1, 0), 2, after))
    hops[1].wait_recv()
    mine[group_of(3, 1)] += recv1[3]
    hops.append(ring(group_of(3, 1), 5, before))
    for hop in hops[2:]:
        hop.wait_recv()
    s1[pl.ds(0, 2)] = mine[group_of(0, 0)] + recv1[2] + recv1[4]
    s1[pl.ds(2, 2)] = mine[group_of(0, 1)] + recv1[1] + recv1[5]

    seconds = {}
    for off in near_last:
        seconds[off] = go(remote(
            s1.at[lax.rem(p2 + off, SIDE)], recv2.at[off - 1],
            c_send.at[off - 1], c_recv.at[off - 1], second_peer(off),
        ))
    total = s1[p2]
    for off in near_first:
        seconds[off].wait_recv()
        total = total + recv2[off - 1]
    s2[...] = total

    far_first = (4, 3, 5, 2, 6, 1, 7)
    far_last = far_first[::-1]

    def eight(i):
        return pl.ds(pl.multiple_of(8 * i, 8), 8)

    reps = {}
    for off in far_first:
        reps[off] = go(remote(
            s2.at[eight(lax.rem(z + off, REPS)), :], recv3.at[off - 1],
            z_send.at[off - 1], z_recv.at[off - 1], rep_peer(off),
        ))
    total = s2[eight(z), :]
    for off in far_last:
        reps[off].wait_recv()
        total = total + recv3[off - 1]

    whole[eight(z), :] = total * (1.0 / REPS)
    reps = {}
    for off in far_first:
        reps[off] = go(remote(
            whole.at[eight(z), :], whole.at[eight(z), :],
            gz_send.at[off - 1], gz_recv.at[off - 1], rep_peer(off),
        ))
    for off in far_last:
        reps[off].wait_recv()

    own_block = full.at[c, 4 * p1 + p2]
    own_block[...] = whole[...]
    seconds = {}
    for off in near_last:
        seconds[off] = go(remote(
            own_block, own_block, gb_send.at[off - 1], gb_recv.at[off - 1], second_peer(off)
        ))
    for off in near_first:
        seconds[off].wait_recv()

    def pass_on(off):
        group = full.at[c, pl.ds(4 * lax.rem(p1 + SIDE - off, SIDE), 4)]
        return go(remote(group, group, gs_send.at[off], gs_recv.at[off], sibling))

    lane = lax.broadcasted_iota(jnp.int32, (RANK, 128), 1)
    row = lax.broadcasted_iota(jnp.int32, (RANK, 128), 0)

    def absorb(k, q):
        left = jnp.concatenate([full[k, 4 * q + i] for i in range(4)], axis=1)
        high = left.astype(BF16)
        low = (left - high.astype(F32)).astype(BF16)
        rows = pl.ds(pl.multiple_of(RANK * k, RANK), RANK)
        cols = pl.ds(pl.multiple_of(512 * q, 512), 512)
        lsplit[0, rows, cols] = high
        lsplit[1, rows, cols] = low
        terms = jnp.concatenate([high, low], axis=0)
        part = lax.dot_general(dsplit[k, :, cols], terms, NT, preferred_element_type=F32)
        return part[:HID] + part[HID:]

    def absorb_own(off):
        return absorb(c, lax.rem(p1 + SIDE - off, SIDE))

    def absorb_other(off):
        passed[off].wait_recv()
        return absorb(1 - c, lax.rem(p2 + SIDE - off, SIDE))

    own_group = full.at[c, pl.ds(4 * p1, 4)]
    firsts = {}
    for off in near_last:
        firsts[off] = go(remote(
            own_group, own_group, gc_send.at[off - 1], gc_recv.at[off - 1], first_peer(off)
        ))
    passed = {0: pass_on(0)}
    prod_own = absorb_own(0)
    prod_other = absorb_other(0)
    for off in near_first:
        firsts[off].wait_recv()
        passed[off] = pass_on(off)
        prod_own = prod_own + absorb_own(off)

    def left_terms(k):
        rows = pl.ds(RANK * k, RANK)
        return jnp.concatenate([lsplit[0, rows, :], lsplit[1, rows, :]], axis=0)

    def packed(part):
        part = part + pltpu.roll(part, RANK, 1)
        wide = lax.broadcasted_iota(jnp.int32, (HID // 2, 128), 1)
        return jnp.where(wide < RANK, part[: HID // 2], part[HID // 2 :])

    def p_rows(i):
        return pl.ds(pl.multiple_of(16 * i, 16), 16)

    def scatter(slot, part):
        psum[slot, pl.ds(0, HID // 2), :] = packed(part)
        psum[slot, pl.ds(HID // 2, 16), :] = jnp.zeros((16, 128), F32)
        out = {}
        for off in far_first:
            n = 7 * slot + off - 1
            out[off] = go(remote(
                psum.at[slot, p_rows(lax.rem(z + off, REPS)), :], recv4.at[slot, off - 1],
                pz_send.at[n], pz_recv.at[n], rep_peer(off),
            ))
        return out

    parts = [scatter(0, prod_own)]
    for off in near_first:
        prod_other = prod_other + absorb_other(off)
    parts.append(scatter(1, prod_other))
    store_left.start()

    tables = []
    for k in range(2):
        terms = left_terms(k)
        gram = lax.dot_general(terms, terms, NT, preferred_element_type=F32)
        gram = gram[:RANK] + gram[RANK:]
        gram = gram + pltpu.roll(gram, RANK, 1)
        tables.append(jnp.where(lane < RANK, gram, jnp.where(lane == row + RANK, 1.0, 0.0)))

    def eliminate(j):
        for k in range(2):
            table = tables[k]
            inv = lax.rsqrt(table[j : j + 1, j : j + 1])
            scaled = table[j : j + 1, :] * inv
            factor = jnp.where(row[:, :1] > j, table[:, j : j + 1] * inv, 0.0)
            tables[k] = jnp.where(row == j, scaled, table - factor * scaled)

    for j in range(RANK // 2):
        eliminate(j)

    for slot in range(2):
        total = psum[slot, p_rows(z), :]
        for off in far_last:
            parts[slot][off].wait_recv()
            total = total + recv4[slot, off - 1]
        pfull[slot, p_rows(z), :] = total * (1.0 / REPS)
    reps = {}
    for off in far_first:
        reps[off] = go(remote(
            pfull.at[:, p_rows(z), :], pfull.at[:, p_rows(z), :],
            pg_send.at[off - 1], pg_recv.at[off - 1], rep_peer(off),
        ))

    for j in range(RANK // 2, RANK):
        eliminate(j)

    inverse0 = jnp.where(lane < RANK, pltpu.roll(tables[0], RANK, 1), 0.0)
    inverse1 = jnp.where(lane >= RANK, tables[1], 0.0)
    solve_out[pl.ds(0, RANK), :] = inverse0
    solve_out[pl.ds(RANK, RANK), :] = inverse1
    both = jnp.concatenate([inverse0, inverse1], axis=0)
    solve_out[pl.ds(2 * RANK, 2 * RANK), :] = jnp.dot(
        both.T, both, precision=highest, preferred_element_type=F32
    )

    for off in far_last:
        reps[off].wait_recv()
    own, other = pfull[0, pl.ds(0, HID // 2), :], pfull[1, pl.ds(0, HID // 2), :]
    gate = jnp.where(c == 0, own, other)
    gate = jnp.concatenate([gate, pltpu.roll(gate, RANK, 1)], axis=0)
    raised = jnp.where(c == 0, other, own)
    raised = jnp.concatenate([pltpu.roll(raised, RANK, 1), raised], axis=0)
    wide = lax.broadcasted_iota(jnp.int32, (HID, 128), 1)
    p_out[...] = jnp.where(wide < RANK, gate, raised)

    drain()


AG_SENDS = 30


def step_call(tokens, upstream, weight, feedback, right_factor):
    any_space = pl.BlockSpec(memory_space=pl.ANY)
    vmem = pl.BlockSpec(memory_space=pltpu.VMEM)
    dma = pltpu.SemaphoreType.DMA
    return pl.pallas_call(
        step_kernel,
        name="gather_reduce",
        out_shape=(
            jax.ShapeDtypeStruct((2 * HID, DIM), F32),
            jax.ShapeDtypeStruct((2, 2 * RANK, DIM), BF16),
            jax.ShapeDtypeStruct((256, 128), F32),
            jax.ShapeDtypeStruct((HID, 128), F32),
        ),
        in_specs=[pl.BlockSpec(memory_space=pltpu.HBM)] * 5,
        out_specs=(any_space, any_space, vmem, vmem),
        scratch_shapes=[
            pltpu.VMEM((PAIRS, 4 * CHUNK, DIM), BF16),
            pltpu.VMEM((2 * HID, DIM), F32),
            pltpu.VMEM((2 * HID, DIM), BF16),
            pltpu.VMEM((HID, 32 * CHUNK), BF16),
            pltpu.VMEM((2, RANK, HID), F32),
            pltpu.VMEM((2, 2 * RANK, HID), BF16),
            pltpu.VMEM((2, 2 * HID, DIM), BF16),
            pltpu.VMEM((16, RANK, 128), F32),
            pltpu.VMEM((16, RANK, 128), F32),
            pltpu.VMEM((16, RANK, 128), F32),
            pltpu.VMEM((6, 2, RANK, 128), F32),
            pltpu.VMEM((4, RANK, 128), F32),
            pltpu.VMEM((3, RANK, 128), F32),
            pltpu.VMEM((RANK, 128), F32),
            pltpu.VMEM((7, 8, 128), F32),
            pltpu.VMEM((RANK, 128), F32),
            pltpu.VMEM((2, 16, RANK, 128), F32),
            pltpu.VMEM((2, 2 * RANK, DIM), BF16),
            pltpu.VMEM((2, 128, 128), F32),
            pltpu.VMEM((2, 7, 16, 128), F32),
            pltpu.VMEM((2, 128, 128), F32),
            dma((5,)), dma((2,)),
            dma((AG_SENDS,)), dma((UNITS, 2)), dma((UNITS,)), dma((UNITS,)),
            dma((4,)), dma((4,)), dma((6,)), dma((6,)), dma((3,)), dma((3,)), dma((7,)), dma((7,)),
            dma((7,)), dma((7,)), dma((3,)), dma((3,)), dma((3,)), dma((3,)), dma((4,)), dma((4,)),
            dma((14,)), dma((14,)), dma((7,)), dma((7,)), pltpu.SemaphoreType.REGULAR((2,)),
        ],
        compiler_params=pltpu.CompilerParams(
            collective_id=0, has_side_effects=True, vmem_limit_bytes=44 * 1024 * 1024
        ),
    )(
        *(
            pltpu.with_memory_space_constraint(array, pltpu.HBM)
            for array in (
                tokens.reshape(CHUNK, DIM),
                upstream.reshape(HID, 32 * CHUNK),
                weight.reshape(2 * HID, DIM),
                feedback.reshape(2 * HID, DIM),
                jnp.swapaxes(right_factor, 1, 2),
            )
        )
    )


COLS = 512
SLAB = DIM // REPS


def finish_kernel(
    delta, left, solve, p, mom, w, fb_out, mom_out, w_out, right_out,
    fb, mom_next, w_next, right, coef, out_sem,
):
    z = lax.axis_index("rep")
    slab = pl.ds(pl.multiple_of(SLAB * z, SLAB), SLAB)
    stores = []

    def store(src, dst):
        stores.append(pltpu.make_async_copy(src, dst, out_sem.at[len(stores)]))
        stores[-1].start()

    rows = p[...]
    weights = lax.dot_general(
        rows, solve[pl.ds(2 * RANK, 2 * RANK), :], NT,
        precision=highest, preferred_element_type=F32,
    )
    lane = lax.broadcasted_iota(jnp.int32, (HID, 128), 1)
    for k in range(2):
        own = jnp.where((lane < RANK) == (k == 0), weights, 0.0)
        high = own.astype(BF16)
        low = (own - high.astype(F32)).astype(BF16)
        coef[pl.ds(k * HID, HID), :] = jnp.concatenate([high, high, low], axis=1)

    def approx_at(cols):
        return jnp.dot(
            coef[:, : 4 * RANK], left[:, cols], preferred_element_type=F32
        ) + jnp.dot(
            coef[:, 4 * RANK :], left[pl.ds(0, 2 * RANK), cols], preferred_element_type=F32
        )

    for j in range(DIM // COLS):
        cols = pl.ds(COLS * j, COLS)
        approx = approx_at(cols)
        for k in range(2):
            fb[k, :, cols] = delta[k, :, cols] - approx[k * HID : (k + 1) * HID]
        store(fb.at[:, :, cols], fb_out.at[:, :, cols])
        if j == 0:
            turned = lax.dot_general(
                solve[pl.ds(0, 2 * RANK), :], rows, NT,
                precision=highest, preferred_element_type=F32,
            )
            right[0] = turned[:RANK]
            right[1] = turned[RANK:]
            store(right, right_out)
            approx = approx_at(slab)
            for k in range(2):
                moved = momentum_decay * mom[k] + approx[k * HID : (k + 1) * HID]
                mom_next[k] = moved
                w_next[k] = (w[k, :, slab].astype(F32) - step_rate * moved).astype(BF16)
            store(mom_next, mom_out)
            store(w_next, w_out)
    for copy in stores:
        copy.wait()


def finish_call(*arrays):
    dma = pltpu.SemaphoreType.DMA
    return pl.pallas_call(
        finish_kernel,
        name="finish",
        in_specs=[pl.BlockSpec(memory_space=pltpu.VMEM)] * 6,
        out_specs=(pl.BlockSpec(memory_space=pl.ANY),) * 4,
        out_shape=(
            jax.ShapeDtypeStruct((2, HID, DIM), F32),
            jax.ShapeDtypeStruct((2, HID, SLAB), F32),
            jax.ShapeDtypeStruct((2, HID, SLAB), BF16),
            jax.ShapeDtypeStruct((2, RANK, HID), F32),
        ),
        scratch_shapes=[
            pltpu.VMEM((2, HID, DIM), F32),
            pltpu.VMEM((2, HID, SLAB), F32),
            pltpu.VMEM((2, HID, SLAB), BF16),
            pltpu.VMEM((2, RANK, HID), F32),
            pltpu.VMEM((2 * HID, 6 * RANK), BF16),
            dma((DIM // COLS + 3,)),
        ],
        compiler_params=pltpu.CompilerParams(vmem_limit_bytes=24 * 1024 * 1024),
    )(*(pltpu.with_memory_space_constraint(array, pltpu.VMEM) for array in arrays))


def per_device(tokens, upstream, weight, feedback, momentum, right_factor):
    delta, left, solve, p = step_call(tokens, upstream, weight, feedback, right_factor)
    feedback_next, momentum_next, weight_next, right_next = finish_call(
        delta.reshape(2, HID, DIM), left.reshape(4 * RANK, DIM), solve, p, momentum, weight
    )
    return (feedback_next[None], momentum_next, weight_next, jnp.swapaxes(right_next, 1, 2))


def solution(mesh):
    placed = (
        P("rep", "fsdp", None),
        P("rep", "fsdp", None),
        P(None, "fsdp", None),
        P("rep", None, "fsdp", None),
        P(None, "fsdp", "rep"),
        P(None, "fsdp", None),
    )
    return jax.shard_map(
        per_device,
        mesh=mesh,
        in_specs=placed,
        out_specs=(
            P("rep", None, "fsdp", None),
            P(None, "fsdp", "rep"),
            P(None, "fsdp", "rep"),
            P(None, "fsdp", None),
        ),
        check_vma=False,
    )
```

```python
import functools

import jax
import jax.numpy as jnp
from jax import lax
from jax.experimental import pallas as pl
from jax.experimental.pallas import tpu as pltpu
from jax.sharding import PartitionSpec as P

momentum_decay = 0.9
step_rate = 0.05
highest = lax.Precision.HIGHEST
MESH = pl.DeviceIdType.MESH
F32 = jnp.float32
BF16 = jnp.bfloat16

CHUNK = 128
HALF = 64
DIM = 2048
HID = 224
RANK = 64
REPS = 8
SIDE = 4
NT = (((1,), (1,)), ((), ()))

ORDER = [
    (0, 0), (3, 0),
    (1, 0), (0, 3),
    (0, 1), (2, 0),
    (0, 2), (3, 3),
    (1, 1), (1, 3),
    (3, 1), (2, 3),
    (2, 1), (3, 2),
    (1, 2), (2, 2),
]
UNIT = {pos: i for i, pos in enumerate(ORDER)}
UNITS = len(ORDER)
PAIRS = UNITS // 2


def pick(table, u):
    out = jnp.int32(0)
    for i, v in enumerate(table):
        if v:
            out = out + jnp.where(u == i, jnp.int32(v), jnp.int32(0))
    return out


def step_kernel(
    tok_hbm, up_hbm, w_hbm, fb_hbm, rf_hbm,
    delta_out, left_out, solve_out, p_out,
    slots, acc, w, up, rf, r2t, dsplit,
    snd_sib, rcv_sib, mine, recv1, s1, recv2, s2, recv3, whole, full, lsplit, psum, recv4, pfull,
    in_sem, out_sem, ag_send, ag_recv, sib_send, sib_recv,
    a_send, a_recv, b_send, b_recv, c_send, c_recv, z_send, z_recv,
    gz_send, gz_recv, gb_send, gb_recv, gc_send, gc_recv, gs_send, gs_recv,
    pz_send, pz_recv, pg_send, pg_recv, meet_sem,
):
    f = lax.axis_index("fsdp")
    z = lax.axis_index("rep")
    c = lax.rem(f, 2)
    x = lax.rem(lax.div(f, 2), SIDE)
    y = lax.div(f, 2 * SIDE)
    p1 = x * (1 - c) + y * c
    p2 = y * (1 - c) + x * c
    t1 = 2 + 6 * c
    t2 = 8 - 6 * c

    def plane(q1, q2):
        return t1 * lax.rem(p1 + q1, SIDE) + t2 * lax.rem(p2 + q2, SIDE) + c

    def first_peer(off):
        return (plane(off, 0), z)

    def second_peer(off):
        return (plane(0, off), z)

    def rep_peer(off):
        return (f, lax.rem(z + off, REPS))

    sibling = (f + 1 - 2 * c, z)

    def remote(src, dst, ssem, rsem, dev):
        return pltpu.make_async_remote_copy(
            src_ref=src, dst_ref=dst, send_sem=ssem, recv_sem=rsem,
            device_id=dev, device_id_type=MESH,
        )

    load_tok = pltpu.make_async_copy(tok_hbm, slots.at[0, pl.ds(0, CHUNK), :], in_sem.at[0])
    load_tok.start()
    loads = [
        pltpu.make_async_copy(w_hbm, w, in_sem.at[1]),
        pltpu.make_async_copy(up_hbm, up, in_sem.at[2]),
        pltpu.make_async_copy(fb_hbm, acc, in_sem.at[3]),
        pltpu.make_async_copy(rf_hbm, rf, in_sem.at[4]),
    ]
    for copy in loads:
        copy.start()

    barrier = pltpu.get_barrier_semaphore()
    peers = [sibling, first_peer(1), first_peer(3), second_peer(1), second_peer(3)]
    peers += [rep_peer(1), rep_peer(REPS - 1)]

    def meet(turn, off):
        for way in (off, REPS - off):
            pl.semaphore_signal(
                meet_sem.at[turn], inc=1, device_id=rep_peer(way), device_id_type=MESH
            )

    for dev in peers:
        pl.semaphore_signal(barrier, inc=1, device_id=dev, device_id_type=MESH)
    pl.semaphore_wait(barrier, len(peers))
    meet(0, 1)

    started = []

    def piece(d1, d2, h):
        u = UNIT[(d1, d2)]
        return slots.at[u // 2, pl.ds(2 * CHUNK * (u % 2) + HALF * h, HALF), :]

    def send(d1, d2, h, axis, way):
        if axis == 1:
            r1, r2 = (d1 - way) % SIDE, d2
            dev = first_peer(way % SIDE)
        else:
            r1, r2 = d1, (d2 - way) % SIDE
            dev = second_peer(way % SIDE)
        own = d1 == 0 and d2 == 0
        copy = remote(
            tok_hbm.at[pl.ds(HALF * h, HALF), :] if own else piece(d1, d2, h), piece(r1, r2, h),
            ag_send.at[len(started)], ag_recv.at[UNIT[(r1, r2)], h], dev,
        )
        copy.start()
        started.append((d1, d2, h))

    def arrived(d1, d2, h):
        remote(
            piece(d1, d2, h), piece(d1, d2, h),
            ag_send.at[0], ag_recv.at[UNIT[(d1, d2)], h], sibling,
        ).wait_recv()

    def sib_copy(u, half):
        start = 2 * CHUNK * half
        pair = slots.at[lax.div(u, 2)]
        return remote(
            pair.at[pl.ds(start, CHUNK), :], pair.at[pl.ds(start + CHUNK, CHUNK), :],
            sib_send.at[u], sib_recv.at[u], sibling,
        )

    def share(d1, d2):
        u = UNIT[(d1, d2)]
        sib_copy(u, u % 2).start()

    def share_own():
        remote(
            tok_hbm, slots.at[0, pl.ds(CHUNK, CHUNK), :], sib_send.at[0], sib_recv.at[0], sibling
        ).start()

    send(0, 0, 0, 1, 1)
    send(0, 0, 1, 1, -1)
    share_own()
    send(0, 0, 1, 1, 1)
    send(0, 0, 0, 1, -1)
    load_tok.wait()
    for copy in loads:
        copy.wait()

    for k in range(2):
        turned = rf[k]
        high = turned.astype(BF16)
        r2t[k, pl.ds(0, RANK), :] = high
        r2t[k, pl.ds(RANK, RANK), :] = (turned - high.astype(F32)).astype(BF16)

    def actions(step):
        if step == 0:
            arrived(3, 0, 0)
            arrived(1, 0, 1)
            send(3, 0, 0, 1, 1)
            send(1, 0, 1, 1, -1)
            send(0, 0, 0, 2, 1)
            send(0, 0, 1, 2, -1)
            send(0, 0, 1, 2, 1)
            send(0, 0, 0, 2, -1)
            send(3, 0, 0, 2, 1)
            send(1, 0, 1, 2, -1)
            send(1, 0, 1, 2, 1)
            send(3, 0, 0, 2, -1)
            arrived(3, 0, 1)
            arrived(1, 0, 0)
            share(3, 0)
            share(1, 0)
            send(3, 0, 1, 2, 1)
            send(1, 0, 0, 2, -1)
            send(1, 0, 0, 2, 1)
            send(3, 0, 1, 2, -1)
        if step == 1:
            arrived(0, 3, 0)
            arrived(0, 1, 1)
            send(0, 3, 0, 2, 1)
            send(0, 1, 1, 2, -1)
            arrived(0, 3, 1)
            arrived(0, 1, 0)
            share(0, 3)
            share(0, 1)
            arrived(2, 0, 0)
            arrived(2, 0, 1)
            send(2, 0, 0, 2, 1)
            send(2, 0, 1, 2, -1)
            share(2, 0)
        if step == 2:
            arrived(3, 3, 0)
            arrived(1, 1, 1)
            send(3, 3, 0, 2, 1)
            send(1, 1, 1, 2, -1)
            send(2, 0, 1, 2, 1)
            send(2, 0, 0, 2, -1)
            pl.semaphore_wait(meet_sem.at[0], 2)
            meet(1, 2)
        if step == 3:
            arrived(0, 2, 0)
            arrived(0, 2, 1)
            share(0, 2)
            arrived(3, 3, 1)
            arrived(1, 1, 0)
            share(3, 3)
            share(1, 1)
        if step == 4:
            arrived(1, 3, 0)
            arrived(3, 1, 1)
            send(1, 3, 0, 2, 1)
            send(3, 1, 1, 2, -1)
            arrived(1, 3, 1)
            arrived(3, 1, 0)
            share(1, 3)
            share(3, 1)
        if step == 5:
            arrived(2, 3, 0)
            arrived(2, 1, 1)
            send(2, 3, 0, 2, 1)
            send(2, 1, 1, 2, -1)
            arrived(2, 3, 1)
            arrived(2, 1, 0)
            share(2, 3)
            share(2, 1)
            pl.semaphore_wait(meet_sem.at[1], 2)
        if step == 6:
            arrived(3, 2, 0)
            arrived(1, 2, 1)
            arrived(3, 2, 1)
            arrived(1, 2, 0)
            share(3, 2)
            share(1, 2)
        if step == 7:
            arrived(2, 2, 0)
            arrived(2, 2, 1)
            share(2, 2)

    first_of = [d1 for d1, _ in ORDER]
    second_of = [d2 for _, d2 in ORDER]

    def cotangents(u):
        d1, d2 = pick(first_of, u), pick(second_of, u)
        other = t2 * lax.rem(p2 + d1, SIDE) + t1 * lax.rem(p1 + d2, SIDE) + (1 - c)
        return [
            up[:, pl.ds(pl.multiple_of(dev * CHUNK, CHUNK), CHUNK)]
            for dev in (plane(d1, d2), other)
        ]

    def pair_step(step, carry):
        for i in range(PAIRS):
            @pl.when(step == i)
            def _(i=i):
                actions(i)

        for half in range(2):
            sib_copy(2 * step + half, half).wait_recv()
        cot = jnp.concatenate(cotangents(2 * step) + cotangents(2 * step + 1), axis=1).astype(F32)
        rows = slots[step]
        pre = lax.dot_general(w[...], rows, NT, preferred_element_type=F32)
        gate_pre, up_pre = pre[:HID], pre[HID:]
        sig = jax.nn.sigmoid(gate_pre)
        grad_gate = (cot * up_pre * (sig * (1.0 + gate_pre * (1.0 - sig)))).astype(BF16)
        grad_up = (cot * (gate_pre * sig)).astype(BF16)
        grads = jnp.concatenate([grad_gate, grad_up], axis=0)
        acc[...] += jnp.dot(grads, rows, preferred_element_type=F32)
        return carry

    lax.fori_loop(0, PAIRS, pair_step, 0)
    pending = []

    def go(copy):
        copy.start()
        pending.append(copy)
        return copy

    def drain():
        for i, (d1, d2, h) in enumerate(started):
            remote(
                piece(d1, d2, h), piece(d1, d2, h), ag_send.at[i], ag_recv.at[0, 0], sibling
            ).wait_send()
        for u in range(UNITS):
            sib_copy(u, u % 2).wait_send()
        for copy in pending:
            copy.wait_send()
        store_delta.wait()
        store_left.wait()

    store_left = pltpu.make_async_copy(lsplit, left_out, out_sem.at[1])
    store_delta = pltpu.make_async_copy(acc, delta_out, out_sem.at[0])
    store_delta.start()

    def left_part(k, g, dst):
        cols = pl.ds(pl.multiple_of(512 * g, 512), 512)
        block = acc[pl.ds(pl.multiple_of(HID * k, 32), HID), cols]
        high = block.astype(BF16)
        low = (block - high.astype(F32)).astype(BF16)
        dsplit[k, pl.ds(0, HID), cols] = high
        dsplit[k, pl.ds(HID, HID), cols] = low
        both = jnp.dot(r2t[k], high, preferred_element_type=F32)
        part = both[:RANK] + both[RANK:]
        part = part + jnp.dot(r2t[k, pl.ds(0, RANK), :], low, preferred_element_type=F32)
        for i in range(4):
            dst[4 * g + i] = part[:, 128 * i : 128 * (i + 1)]

    near_last = (2, 1, 3)
    near_first = (1, 3, 2)
    swaps = {}
    for n, off in enumerate(near_last + (0,)):
        g = lax.rem(p2 + off, SIDE)
        left_part(1 - c, g, snd_sib)
        group = pl.ds(4 * g, 4)
        swaps[off] = go(
            remote(snd_sib.at[group], rcv_sib.at[group], a_send.at[n], a_recv.at[n], sibling)
        )

    after, before = first_peer(1), first_peer(3)

    def group_of(off, half):
        return pl.ds(4 * lax.rem(p1 + off, SIDE) + 2 * half, 2)

    def add_sibling(off):
        q = lax.rem(p1 + off, SIDE)
        left_part(c, q, mine)
        swaps[off].wait_recv()
        group = pl.ds(4 * q, 4)
        mine[group] += rcv_sib[group]

    def ring(group, slot, dev):
        return go(remote(mine.at[group], recv1.at[slot], b_send.at[slot], b_recv.at[slot], dev))

    add_sibling(2)
    hops = [ring(group_of(2, 0), 0, after), ring(group_of(2, 1), 3, before)]
    add_sibling(1)
    hops.append(ring(group_of(1, 1), 1, after))
    add_sibling(3)
    hops.append(ring(group_of(3, 0), 4, before))
    add_sibling(0)
    hops[0].wait_recv()
    mine[group_of(1, 0)] += recv1[0]
    hops.append(ring(group_of(1, 0), 2, after))
    hops[1].wait_recv()
    mine[group_of(3, 1)] += recv1[3]
    hops.append(ring(group_of(3, 1), 5, before))
    for hop in hops[2:]:
        hop.wait_recv()
    s1[pl.ds(0, 2)] = mine[group_of(0, 0)] + recv1[2] + recv1[4]
    s1[pl.ds(2, 2)] = mine[group_of(0, 1)] + recv1[1] + recv1[5]

    seconds = {}
    for off in near_last:
        seconds[off] = go(remote(
            s1.at[lax.rem(p2 + off, SIDE)], recv2.at[off - 1],
            c_send.at[off - 1], c_recv.at[off - 1], second_peer(off),
        ))
    total = s1[p2]
    for off in near_first:
        seconds[off].wait_recv()
        total = total + recv2[off - 1]
    s2[...] = total

    far_first = (4, 3, 5, 2, 6, 1, 7)
    far_last = far_first[::-1]

    def eight(i):
        return pl.ds(pl.multiple_of(8 * i, 8), 8)

    reps = {}
    for off in far_first:
        reps[off] = go(remote(
            s2.at[eight(lax.rem(z + off, REPS)), :], recv3.at[off - 1],
            z_send.at[off - 1], z_recv.at[off - 1], rep_peer(off),
        ))
    total = s2[eight(z), :]
    for off in far_last:
        reps[off].wait_recv()
        total = total + recv3[off - 1]

    whole[eight(z), :] = total * (1.0 / REPS)
    reps = {}
    for off in far_first:
        reps[off] = go(remote(
            whole.at[eight(z), :], whole.at[eight(z), :],
            gz_send.at[off - 1], gz_recv.at[off - 1], rep_peer(off),
        ))
    for off in far_last:
        reps[off].wait_recv()

    own_block = full.at[c, 4 * p1 + p2]
    own_block[...] = whole[...]
    seconds = {}
    for off in near_last:
        seconds[off] = go(remote(
            own_block, own_block, gb_send.at[off - 1], gb_recv.at[off - 1], second_peer(off)
        ))
    for off in near_first:
        seconds[off].wait_recv()

    def pass_on(off):
        group = full.at[c, pl.ds(4 * lax.rem(p1 + SIDE - off, SIDE), 4)]
        return go(remote(group, group, gs_send.at[off], gs_recv.at[off], sibling))

    lane = lax.broadcasted_iota(jnp.int32, (RANK, 128), 1)
    row = lax.broadcasted_iota(jnp.int32, (RANK, 128), 0)

    def absorb(k, q):
        left = jnp.concatenate([full[k, 4 * q + i] for i in range(4)], axis=1)
        high = left.astype(BF16)
        low = (left - high.astype(F32)).astype(BF16)
        rows = pl.ds(pl.multiple_of(RANK * k, RANK), RANK)
        cols = pl.ds(pl.multiple_of(512 * q, 512), 512)
        lsplit[0, rows, cols] = high
        lsplit[1, rows, cols] = low
        terms = jnp.concatenate([high, low], axis=0)
        part = lax.dot_general(dsplit[k, :, cols], terms, NT, preferred_element_type=F32)
        return part[:HID] + part[HID:]

    def absorb_own(off):
        return absorb(c, lax.rem(p1 + SIDE - off, SIDE))

    def absorb_other(off):
        passed[off].wait_recv()
        return absorb(1 - c, lax.rem(p2 + SIDE - off, SIDE))

    own_group = full.at[c, pl.ds(4 * p1, 4)]
    firsts = {}
    for off in near_last:
        firsts[off] = go(remote(
            own_group, own_group, gc_send.at[off - 1], gc_recv.at[off - 1], first_peer(off)
        ))
    passed = {0: pass_on(0)}
    prod_own = absorb_own(0)
    prod_other = absorb_other(0)
    for off in near_first:
        firsts[off].wait_recv()
        passed[off] = pass_on(off)
        prod_own = prod_own + absorb_own(off)

    def left_terms(k):
        rows = pl.ds(RANK * k, RANK)
        return jnp.concatenate([lsplit[0, rows, :], lsplit[1, rows, :]], axis=0)

    def packed(part):
        part = part + pltpu.roll(part, RANK, 1)
        wide = lax.broadcasted_iota(jnp.int32, (HID // 2, 128), 1)
        return jnp.where(wide < RANK, part[: HID // 2], part[HID // 2 :])

    def p_rows(i):
        return pl.ds(pl.multiple_of(16 * i, 16), 16)

    def scatter(slot, part):
        psum[slot, pl.ds(0, HID // 2), :] = packed(part)
        psum[slot, pl.ds(HID // 2, 16), :] = jnp.zeros((16, 128), F32)
        out = {}
        for off in far_first:
            n = 7 * slot + off - 1
            out[off] = go(remote(
                psum.at[slot, p_rows(lax.rem(z + off, REPS)), :], recv4.at[slot, off - 1],
                pz_send.at[n], pz_recv.at[n], rep_peer(off),
            ))
        return out

    parts = [scatter(0, prod_own)]
    for off in near_first:
        prod_other = prod_other + absorb_other(off)
    parts.append(scatter(1, prod_other))
    store_left.start()

    tables = []
    for k in range(2):
        terms = left_terms(k)
        gram = lax.dot_general(terms, terms, NT, preferred_element_type=F32)
        gram = gram[:RANK] + gram[RANK:]
        gram = gram + pltpu.roll(gram, RANK, 1)
        tables.append(jnp.where(lane < RANK, gram, jnp.where(lane == row + RANK, 1.0, 0.0)))

    def eliminate(j):
        for k in range(2):
            table = tables[k]
            inv = lax.rsqrt(table[j : j + 1, j : j + 1])
            scaled = table[j : j + 1, :] * inv
            factor = jnp.where(row[:, :1] > j, table[:, j : j + 1] * inv, 0.0)
            tables[k] = jnp.where(row == j, scaled, table - factor * scaled)

    for j in range(RANK // 2):
        eliminate(j)

    def spread_mean(slot):
        total = psum[slot, p_rows(z), :]
        for off in far_last:
            parts[slot][off].wait_recv()
            total = total + recv4[slot, off - 1]
        pfull[slot, p_rows(z), :] = total * (1.0 / REPS)
        piece_p = pfull.at[slot, p_rows(z), :]
        out = []
        for off in far_first:
            n = 7 * slot + off - 1
            out.append(go(remote(piece_p, piece_p, pg_send.at[n], pg_recv.at[n], rep_peer(off))))
        return out

    means = spread_mean(0)
    for j in range(RANK // 2, 3 * RANK // 4):
        eliminate(j)
    means += spread_mean(1)
    for j in range(3 * RANK // 4, RANK):
        eliminate(j)

    inverse0 = jnp.where(lane < RANK, pltpu.roll(tables[0], RANK, 1), 0.0)
    inverse1 = jnp.where(lane >= RANK, tables[1], 0.0)
    solve_out[pl.ds(0, RANK), :] = inverse0
    solve_out[pl.ds(RANK, RANK), :] = inverse1
    both = jnp.concatenate([inverse0, inverse1], axis=0)
    solve_out[pl.ds(2 * RANK, 2 * RANK), :] = jnp.dot(
        both.T, both, precision=highest, preferred_element_type=F32
    )

    for copy in means:
        copy.wait_recv()
    own, other = pfull[0, pl.ds(0, HID // 2), :], pfull[1, pl.ds(0, HID // 2), :]
    gate = jnp.where(c == 0, own, other)
    gate = jnp.concatenate([gate, pltpu.roll(gate, RANK, 1)], axis=0)
    raised = jnp.where(c == 0, other, own)
    raised = jnp.concatenate([pltpu.roll(raised, RANK, 1), raised], axis=0)
    wide = lax.broadcasted_iota(jnp.int32, (HID, 128), 1)
    p_out[...] = jnp.where(wide < RANK, gate, raised)

    drain()


AG_SENDS = 30


def step_call(tokens, upstream, weight, feedback, right_factor):
    any_space = pl.BlockSpec(memory_space=pl.ANY)
    vmem = pl.BlockSpec(memory_space=pltpu.VMEM)
    dma = pltpu.SemaphoreType.DMA
    return pl.pallas_call(
        step_kernel,
        name="gather_reduce",
        out_shape=(
            jax.ShapeDtypeStruct((2 * HID, DIM), F32),
            jax.ShapeDtypeStruct((2, 2 * RANK, DIM), BF16),
            jax.ShapeDtypeStruct((256, 128), F32),
            jax.ShapeDtypeStruct((HID, 128), F32),
        ),
        in_specs=[pl.BlockSpec(memory_space=pltpu.HBM)] * 5,
        out_specs=(any_space, any_space, vmem, vmem),
        scratch_shapes=[
            pltpu.VMEM((PAIRS, 4 * CHUNK, DIM), BF16),
            pltpu.VMEM((2 * HID, DIM), F32),
            pltpu.VMEM((2 * HID, DIM), BF16),
            pltpu.VMEM((HID, 32 * CHUNK), BF16),
            pltpu.VMEM((2, RANK, HID), F32),
            pltpu.VMEM((2, 2 * RANK, HID), BF16),
            pltpu.VMEM((2, 2 * HID, DIM), BF16),
            pltpu.VMEM((16, RANK, 128), F32),
            pltpu.VMEM((16, RANK, 128), F32),
            pltpu.VMEM((16, RANK, 128), F32),
            pltpu.VMEM((6, 2, RANK, 128), F32),
            pltpu.VMEM((4, RANK, 128), F32),
            pltpu.VMEM((3, RANK, 128), F32),
            pltpu.VMEM((RANK, 128), F32),
            pltpu.VMEM((7, 8, 128), F32),
            pltpu.VMEM((RANK, 128), F32),
            pltpu.VMEM((2, 16, RANK, 128), F32),
            pltpu.VMEM((2, 2 * RANK, DIM), BF16),
            pltpu.VMEM((2, 128, 128), F32),
            pltpu.VMEM((2, 7, 16, 128), F32),
            pltpu.VMEM((2, 128, 128), F32),
            dma((5,)), dma((2,)),
            dma((AG_SENDS,)), dma((UNITS, 2)), dma((UNITS,)), dma((UNITS,)),
            dma((4,)), dma((4,)), dma((6,)), dma((6,)), dma((3,)), dma((3,)), dma((7,)), dma((7,)),
            dma((7,)), dma((7,)), dma((3,)), dma((3,)), dma((3,)), dma((3,)), dma((4,)), dma((4,)),
            dma((14,)), dma((14,)), dma((14,)), dma((14,)), pltpu.SemaphoreType.REGULAR((2,)),
        ],
        compiler_params=pltpu.CompilerParams(
            collective_id=0, has_side_effects=True, vmem_limit_bytes=44 * 1024 * 1024
        ),
    )(
        *(
            pltpu.with_memory_space_constraint(array, pltpu.HBM)
            for array in (
                tokens.reshape(CHUNK, DIM),
                upstream.reshape(HID, 32 * CHUNK),
                weight.reshape(2 * HID, DIM),
                feedback.reshape(2 * HID, DIM),
                jnp.swapaxes(right_factor, 1, 2),
            )
        )
    )


COLS = 512
SLAB = DIM // REPS


def finish_kernel(
    delta, left, solve, p, mom, w, fb_out, mom_out, w_out, right_out,
    fb, mom_next, w_next, right, coef, out_sem,
):
    z = lax.axis_index("rep")
    slab = pl.ds(pl.multiple_of(SLAB * z, SLAB), SLAB)
    stores = []

    def store(src, dst):
        stores.append(pltpu.make_async_copy(src, dst, out_sem.at[len(stores)]))
        stores[-1].start()

    rows = p[...]
    weights = lax.dot_general(
        rows, solve[pl.ds(2 * RANK, 2 * RANK), :], NT,
        precision=highest, preferred_element_type=F32,
    )
    lane = lax.broadcasted_iota(jnp.int32, (HID, 128), 1)
    for k in range(2):
        own = jnp.where((lane < RANK) == (k == 0), weights, 0.0)
        high = own.astype(BF16)
        low = (own - high.astype(F32)).astype(BF16)
        coef[pl.ds(k * HID, HID), :] = jnp.concatenate([high, high, low], axis=1)

    def approx_at(cols):
        return jnp.dot(
            coef[:, : 4 * RANK], left[:, cols], preferred_element_type=F32
        ) + jnp.dot(
            coef[:, 4 * RANK :], left[pl.ds(0, 2 * RANK), cols], preferred_element_type=F32
        )

    for j in range(DIM // COLS):
        cols = pl.ds(COLS * j, COLS)
        approx = approx_at(cols)
        for k in range(2):
            fb[k, :, cols] = delta[k, :, cols] - approx[k * HID : (k + 1) * HID]
        store(fb.at[:, :, cols], fb_out.at[:, :, cols])
        if j == 0:
            turned = lax.dot_general(
                solve[pl.ds(0, 2 * RANK), :], rows, NT,
                precision=highest, preferred_element_type=F32,
            )
            right[0] = turned[:RANK]
            right[1] = turned[RANK:]
            store(right, right_out)
            approx = approx_at(slab)
            for k in range(2):
                moved = momentum_decay * mom[k] + approx[k * HID : (k + 1) * HID]
                mom_next[k] = moved
                w_next[k] = (w[k, :, slab].astype(F32) - step_rate * moved).astype(BF16)
            store(mom_next, mom_out)
            store(w_next, w_out)
    for copy in stores:
        copy.wait()


def finish_call(*arrays):
    dma = pltpu.SemaphoreType.DMA
    return pl.pallas_call(
        finish_kernel,
        name="finish",
        in_specs=[pl.BlockSpec(memory_space=pltpu.VMEM)] * 6,
        out_specs=(pl.BlockSpec(memory_space=pl.ANY),) * 4,
        out_shape=(
            jax.ShapeDtypeStruct((2, HID, DIM), F32),
            jax.ShapeDtypeStruct((2, HID, SLAB), F32),
            jax.ShapeDtypeStruct((2, HID, SLAB), BF16),
            jax.ShapeDtypeStruct((2, RANK, HID), F32),
        ),
        scratch_shapes=[
            pltpu.VMEM((2, HID, DIM), F32),
            pltpu.VMEM((2, HID, SLAB), F32),
            pltpu.VMEM((2, HID, SLAB), BF16),
            pltpu.VMEM((2, RANK, HID), F32),
            pltpu.VMEM((2 * HID, 6 * RANK), BF16),
            dma((DIM // COLS + 3,)),
        ],
        compiler_params=pltpu.CompilerParams(vmem_limit_bytes=24 * 1024 * 1024),
    )(*(pltpu.with_memory_space_constraint(array, pltpu.VMEM) for array in arrays))


def per_device(tokens, upstream, weight, feedback, momentum, right_factor):
    delta, left, solve, p = step_call(tokens, upstream, weight, feedback, right_factor)
    feedback_next, momentum_next, weight_next, right_next = finish_call(
        delta.reshape(2, HID, DIM), left.reshape(4 * RANK, DIM), solve, p, momentum, weight
    )
    return (feedback_next[None], momentum_next, weight_next, jnp.swapaxes(right_next, 1, 2))


def solution(mesh):
    placed = (
        P("rep", "fsdp", None),
        P("rep", "fsdp", None),
        P(None, "fsdp", None),
        P("rep", None, "fsdp", None),
        P(None, "fsdp", "rep"),
        P(None, "fsdp", None),
    )
    return jax.shard_map(
        per_device,
        mesh=mesh,
        in_specs=placed,
        out_specs=(
            P("rep", None, "fsdp", None),
            P(None, "fsdp", "rep"),
            P(None, "fsdp", "rep"),
            P(None, "fsdp", None),
        ),
        check_vma=False,
    )
```
